768 devices in a mesh: section: 48 (over y_hi, z), tensor: 16 (over y_lo, x, core).
Axes of the slice: x: 4, y: 8 (y_hi: 4, y_lo: 2; y = y_hi * 2 + y_lo), z: 12, core: 2. Of those that a mesh axis runs over, the one named last changes fastest.
Arguments:
- layer_input: bfloat16 [48, 512, 6144], P('section', None, 'tensor'), may hold values from -200 to 200
- grad_input: bfloat16 [48, 512, 6144], P('section', None, 'tensor'), may hold values from -8 to 8
- stashed: bfloat16 [48, 2, 512, 6144], P('section', None, None, 'tensor'), may hold values from -200 to 200
- eviction: int32 [48], P('section'), may hold values from 0 to 1, as said below
- query_gain: float32 [48, 6144], P('section', 'tensor'), may hold values from 0.5 to 2
- key_gain: float32 [48, 6144], P('section', 'tensor'), may hold values from 0.5 to 2
Outputs:
- layer_output: bfloat16 [48, 512, 6144], P('section', None, 'tensor')
- grad_output: bfloat16 [48, 512, 6144], P('section', None, 'tensor')
The draws below stay inside these ranges and needn't reach their ends.
Inputs may be any that keep to these rules, and one draw needn't show every extreme that they name: `eviction`: section 0 always evicts.
All inputs are finite; a program needn't handle non-finite values.
Results may differ from the reference program's by a relative error of at most 0.0078.
Values may be sent and summed in bfloat16 or wider, within the bound.
A program may use at most 32 MiB of HBM per device.

```python
import math
import jax
import jax.numpy as jnp
from jax import lax

HEADS = 48
HDIM = 128
SEQ = 512
DW = 6144
SECTIONS = 48


def shared_direction(key):
    return jnp.clip(jax.random.normal(jax.random.fold_in(key, 77), (SECTIONS, DW), jnp.float32), -4.0, 4.0)


def column_scale(key):
    rising = jnp.exp(math.log(3.0) * jnp.arange(DW, dtype=jnp.float32) / DW)
    spread = jnp.exp(jax.random.uniform(jax.random.fold_in(key, 78), (DW,), jnp.float32, math.log(0.3), math.log(3.0)))
    return rising * spread / 1.7


def activation_block(key, label, count):
    own_key = jax.random.fold_in(key, label)
    shape = (SECTIONS, count, SEQ, DW)
    noise = jnp.clip(jax.random.normal(jax.random.fold_in(own_key, 1), shape, jnp.float32), -5.0, 5.0)
    weight_common = 0.8
    common = shared_direction(key)[:, None, None, :]
    row_scale = jnp.exp(jax.random.uniform(jax.random.fold_in(own_key, 2), (SECTIONS, count, SEQ, 1), jnp.float32, math.log(0.3), math.log(3.0)))
    values = (noise + weight_common * common) * row_scale * column_scale(key)
    return jnp.clip(values, -200.0, 200.0)


def draw_layer_input(key, part):
    return activation_block(key, 21, 1)[:, 0].astype(jnp.bfloat16)


def draw_stashed(key, part):
    return activation_block(key, 31, 2).astype(jnp.bfloat16)


def draw_grad_input(key, part):
    own_key = jax.random.fold_in(key, 41)
    shape = (SECTIONS, SEQ, DW)
    noise = jnp.clip(jax.random.normal(own_key, shape, jnp.float32), -5.0, 5.0)
    weight_common = 0.8
    values = noise + weight_common * shared_direction(key)[:, None, :]
    return jnp.clip(values, -8.0, 8.0).astype(jnp.bfloat16)


def draw_eviction(key, part):
    plan = jax.random.randint(jax.random.fold_in(key, 51), (SECTIONS,), 0, 2).astype(jnp.int32)
    first = (jnp.arange(SECTIONS) == 0).astype(jnp.int32)
    return jnp.maximum(plan, first).astype(jnp.int32)


def level_of(rng, dims, split, low, largest):
    level = 1.0
    for dim, shards_of in split:
        steps = jax.random.uniform(jax.random.fold_in(jax.random.fold_in(rng, 6), dim), (shards_of,), jnp.float32, low / len(split), largest / len(split))
        level = level * jnp.repeat(jnp.exp(steps), dims[dim] // shards_of).reshape((-1,) + (1,) * (len(dims) - 1 - dim))
    return level


def setup_inputs(seed: int = 0) -> dict:
    streams_of = jax.random.split(jax.random.key(seed), 7)
    layer_input = draw_layer_input(jax.random.fold_in(streams_of[6], 71), 0)
    grad_input = draw_grad_input(jax.random.fold_in(streams_of[6], 71), 0)
    stashed = draw_stashed(jax.random.fold_in(streams_of[6], 71), 0)
    eviction = draw_eviction(jax.random.fold_in(streams_of[6], 71), 0)
    query_gain = jnp.clip(jnp.exp(math.log(2.0) - 1.3862944 * jax.random.uniform(streams_of[4], (SECTIONS, DW), jnp.float32) ** level_of(streams_of[4], (SECTIONS, DW), ((0, 48), (1, 16)), -0.2, 0.2)), 0.5, 2.0)
    key_gain = jnp.clip(jnp.exp(math.log(2.0) - 1.3862944 * jax.random.uniform(streams_of[5], (SECTIONS, DW), jnp.float32) ** level_of(streams_of[5], (SECTIONS, DW), ((0, 48), (1, 16)), -0.2, 0.2)), 0.5, 2.0)
    return {"layer_input": layer_input, "grad_input": grad_input, "stashed": stashed, "eviction": eviction, "query_gain": query_gain, "key_gain": key_gain}


EPSILON = 1e-05

def normalize(activations, gain_query, gain_key):
    widened = activations.astype(jnp.float32)
    factor = lax.rsqrt(lax.optimization_barrier(jnp.mean(widened * widened, axis=-1)) + EPSILON)
    normed = widened * factor[:, None]
    queries = (normed * gain_query).astype(jnp.bfloat16)
    keys_all = (normed * gain_key).astype(jnp.bfloat16)
    values = normed.astype(jnp.bfloat16)
    return (widened, factor, queries, keys_all, values)

def split_heads(matrix):
    return matrix.astype(jnp.float32).reshape(SEQ, HEADS, HDIM)

def attention_weights(query_heads, key_heads):
    scores = jnp.einsum('qhd,khd->hqk', query_heads, key_heads) * (1.0 / math.sqrt(HDIM))
    causal = jnp.arange(SEQ)[:, None] >= jnp.arange(SEQ)[None, :]
    scores = jnp.where(causal[None], scores, -1e+30)
    shifted = scores - lax.optimization_barrier(jnp.max(scores, axis=-1, keepdims=True))
    exponent = jnp.exp(shifted)
    return exponent / lax.optimization_barrier(jnp.sum(exponent, axis=-1, keepdims=True))

def forward_layer(activations, gain_query, gain_key):
    widened, factor, queries, keys_all, values = normalize(activations, gain_query, gain_key)
    weights = attention_weights(split_heads(queries), split_heads(keys_all))
    rounded = weights.astype(jnp.bfloat16).astype(jnp.float32)
    mixed_heads = jnp.einsum('hqk,khd->qhd', rounded, split_heads(values)).reshape(SEQ, DW)
    return (widened + mixed_heads).astype(jnp.bfloat16)

def backward_layer(activations, upstream, gain_query, gain_key):
    widened, factor, queries, keys_all, values = normalize(activations, gain_query, gain_key)
    weights = attention_weights(split_heads(queries), split_heads(keys_all))
    rounded = weights.astype(jnp.bfloat16).astype(jnp.float32)
    grad_heads = split_heads(upstream)
    d_values = jnp.einsum('hqk,qhd->khd', rounded, grad_heads)
    d_weights = jnp.einsum('qhd,khd->hqk', grad_heads, split_heads(values))
    row_delta = lax.optimization_barrier(jnp.sum(weights * d_weights, axis=-1, keepdims=True))
    d_scores = (weights * (d_weights - row_delta) * (1.0 / math.sqrt(HDIM))).astype(jnp.bfloat16).astype(jnp.float32)
    d_queries = jnp.einsum('hqk,khd->qhd', d_scores, split_heads(keys_all))
    d_keys = jnp.einsum('hqk,qhd->khd', d_scores, split_heads(queries))
    d_normed = d_queries.reshape(SEQ, DW) * gain_query + d_keys.reshape(SEQ, DW) * gain_key + d_values.reshape(SEQ, DW)
    inner_sum = lax.optimization_barrier(jnp.sum(d_normed * widened, axis=-1))
    result = upstream.astype(jnp.float32) + factor[:, None] * d_normed - widened * (factor ** 3)[:, None] * inner_sum[:, None] / DW
    return result.astype(jnp.bfloat16)

def reference(layer_input, grad_input, stashed, eviction, query_gain, key_gain):
    half_sections = SECTIONS // 2

    def per_section(index):
        output = forward_layer(layer_input[index], query_gain[index], key_gain[index])
        partner = ((index + half_sections) % SECTIONS).astype(jnp.int32)
        chosen = jnp.where(eviction[index] == 1, stashed[partner, 1], stashed[index, 0])
        result = backward_layer(chosen, grad_input[index], query_gain[index], key_gain[index])
        return (output, result)
    outputs, results = lax.map(per_section, jnp.arange(SECTIONS, dtype=jnp.int32))
    grad_output = jnp.concatenate([results[1:], results[:1]], axis=0)
    return (outputs, grad_output)
```

```python
import functools
import math

import jax
import jax.numpy as jnp
from jax import lax
from jax.experimental import pallas as pl
from jax.experimental.pallas import tpu as pltpu
from jax.sharding import PartitionSpec as P

MESH = pl.DeviceIdType.MESH
HDIM = 128
SEQ = 512
DW = 6144
SECTIONS = 48
PLANES = 12
GROUP = 16
HEADS = 3
BLOCK = 128
LANES = 128
ROWS = SEQ // LANES
CHUNK = 64
CHUNKS = SEQ // CHUNK
EPSILON = 1e-05
SCALE = 1.0 / math.sqrt(HDIM)
EXPONENT = SCALE * math.log2(math.e)
NT = (((1,), (1,)), ((), ()))
TN = (((0,), (0,)), ((), ()))
NN = (((1,), (0,)), ((), ()))


def dot(a, b, dims):
    return lax.dot_general(a, b, dims, preferred_element_type=jnp.float32)


def row_sums(values):
    high = values.astype(jnp.bfloat16)
    low = (values - high.astype(jnp.float32)).astype(jnp.bfloat16)
    ones = jnp.ones((8, values.shape[-1]), jnp.bfloat16)
    return (dot(ones, high, NT) + dot(ones, low, NT))[0:1]


def spread_columns(lane_rows, out_ref):
    for b in range(ROWS):
        block = jnp.broadcast_to(lane_rows[b : b + 1], (LANES, LANES))
        out_ref[pl.ds(b * LANES, LANES), :] = block.T


def block_weights(keys, queries, lo, hi):
    scores = dot(keys[:hi], queries[lo:hi], NT)
    width = hi - lo
    tail = scores[lo:]
    u = lax.broadcasted_iota(jnp.int32, (width, width), 0)
    t = lax.broadcasted_iota(jnp.int32, (width, width), 1)
    tail = jnp.where(u <= t, tail, -1e30)
    scores = tail if lo == 0 else jnp.concatenate([scores[:lo], tail], axis=0)
    top = jnp.max(scores, axis=0, keepdims=True)
    exponent = jnp.exp2((scores - top) * EXPONENT)
    return exponent * (1.0 / jnp.sum(exponent, axis=0, keepdims=True))


def kernel(
    ev_ref, li_ref, g_ref, st_ref, gq_ref, gk_ref,
    lo_ref, out_ref,
    li_v, g_v, own_v, away_v, got_v, x_v, lo_v, dn_v, dk_v, dv_v, dx_v, relay_v,
    part_v, parts_v, extra_v, theirs_v, inner_v, inners_v, f_v, fb_v, cb_v,
    li_s, g_s, own_s, away_s, lo_s,
    stash_ss, stash_rs, sq_ss, sq_rs, ex_ss, ex_rs, in_ss, in_rs,
    dx_ss, dx_rs, rel_rs, fwd_ss,
):
    s, t = lax.axis_index("section"), lax.axis_index("tensor")
    z = lax.rem(s, PLANES)
    first, last = z == 0, z == PLANES - 1

    def section(by):
        return lax.rem(s + (by + SECTIONS), SECTIONS)

    def remote(src, dst, ss, rs, to_s, to_t):
        return pltpu.make_async_remote_copy(
            src_ref=src, dst_ref=dst, send_sem=ss, recv_sem=rs,
            device_id={"section": to_s, "tensor": to_t}, device_id_type=MESH)

    def heads_in(src, dst, sems):
        return [pltpu.make_async_copy(src.at[:, pl.ds(h * HDIM, HDIM)], dst.at[h], sems.at[h]) for h in range(HEADS)]

    away_in = heads_in(st_ref.at[1], away_v, away_s)
    li_in = heads_in(li_ref, li_v, li_s)
    own_in = heads_in(st_ref.at[0], own_v, own_s)
    g_in = heads_in(g_ref, g_v, g_s)
    for c in away_in + li_in + own_in + g_in:
        c.start()

    barrier = pltpu.get_barrier_semaphore()

    def greet(to_s, to_t):
        pl.semaphore_signal(barrier, inc=1, device_id={"section": to_s, "tensor": to_t}, device_id_type=MESH)

    met = (SECTIONS // 2, -1, 1, -PLANES, PLANES, 1 - PLANES, PLANES - 1)
    for by in met:
        greet(section(by), t)
    for by in range(1, GROUP):
        greet(s, lax.rem(t + by, GROUP))

    def squares(ref, slot):
        total = jnp.zeros((1, SEQ), jnp.float32)
        for h in range(HEADS):
            wide = ref[h].astype(jnp.float32)
            total = total + row_sums(wide * wide)
        for b in range(ROWS):
            part_v[pl.ds(slot * ROWS + b, 1), :] = total[:, b * LANES : (b + 1) * LANES]

    for c in away_in:
        c.wait()
    squares(away_v, 2)
    for c in li_in:
        c.wait()
    squares(li_v, 0)
    for c in own_in:
        c.wait()
    squares(own_v, 1)
    for b in range(12, 16):
        part_v[pl.ds(b, 1), :] = jnp.zeros((1, LANES), jnp.float32)

    pl.semaphore_wait(barrier, len(met) + GROUP - 1)

    stash = [remote(away_v.at[h], got_v.at[h], stash_ss.at[h], stash_rs.at[h], section(SECTIONS // 2), t) for h in range(HEADS)]
    shares = [remote(part_v, parts_v.at[i], sq_ss.at[i], sq_rs.at[i], s, lax.rem(t + i, GROUP)) for i in range(1, GROUP)]
    for c in shares:
        c.start()
    for c in stash:
        c.start()
    for c in shares:
        c.wait_recv()
    totals = part_v[...]
    for i in range(1, GROUP):
        totals = totals + parts_v[i]
    extra_v[...] = totals[8:16]
    extra = remote(extra_v, theirs_v, ex_ss, ex_rs, section(SECTIONS // 2), t)
    extra.start()

    def factor_of(total):
        return lax.rsqrt(total / DW + EPSILON)

    spread_columns(factor_of(totals[0:ROWS]), fb_v)
    for c in g_in:
        c.wait()

    def forward(h, carry):
        cols = pl.ds(pl.multiple_of(h * HDIM, HDIM), HDIM)
        wide = li_v[h].astype(jnp.float32)
        normed = wide * fb_v[...]
        queries = (normed * gq_ref[:, cols]).astype(jnp.bfloat16)
        keys = (normed * gk_ref[:, cols]).astype(jnp.bfloat16)
        values = normed.astype(jnp.bfloat16)
        for lo in range(0, SEQ, BLOCK):
            hi = lo + BLOCK
            weights = block_weights(keys, queries, lo, hi).astype(jnp.bfloat16)
            mixed = dot(weights, values[:hi], TN)
            lo_v[h, pl.ds(lo, BLOCK), :] = (wide[lo:hi] + mixed).astype(jnp.bfloat16)
        pltpu.make_async_copy(lo_v.at[h], lo_ref.at[:, cols], lo_s.at[h]).start()
        return carry

    lax.fori_loop(0, HEADS, forward, 0)

    extra.wait_recv()
    evicted = jnp.full((8, LANES), ev_ref[0], jnp.int32) == 1
    own_total = totals[4:8]
    f_v[0:ROWS] = factor_of(jnp.where(evicted[0:ROWS], theirs_v[0:ROWS], own_total))
    spread_columns(f_v[...], fb_v)
    picked = jnp.full((SEQ, HDIM), ev_ref[0], jnp.int32) == 1

    def backward(h, partial):
        cols = pl.ds(pl.multiple_of(h * HDIM, HDIM), HDIM)
        remote(away_v.at[h], got_v.at[h], stash_ss.at[h], stash_rs.at[h], section(SECTIONS // 2), t).wait_recv()
        wide = jnp.where(picked, got_v[h].astype(jnp.float32), own_v[h].astype(jnp.float32))
        x_v[h] = wide.astype(jnp.bfloat16)
        normed = wide * fb_v[...]
        gq, gk = gq_ref[:, cols], gk_ref[:, cols]
        queries = (normed * gq).astype(jnp.bfloat16)
        keys = (normed * gk).astype(jnp.bfloat16)
        values = normed.astype(jnp.bfloat16)
        grads = g_v[h]
        for lo in range(SEQ - BLOCK, -1, -BLOCK):
            hi = lo + BLOCK
            weights = block_weights(keys, queries, lo, hi)
            d_weights = dot(values[:hi], grads[lo:hi], NT)
            delta = jnp.sum(weights * d_weights, axis=0, keepdims=True)
            d_scores = (weights * (d_weights - delta) * SCALE).astype(jnp.bfloat16)
            d_keys = dot(d_scores, queries[lo:hi], NN)
            d_values = dot(weights.astype(jnp.bfloat16), grads[lo:hi], NN)
            if hi == SEQ:
                dk_v[...] = d_keys
                dv_v[...] = d_values
            else:
                dk_v[0:hi] += d_keys
                dv_v[0:hi] += d_values
            dn_v[h, pl.ds(lo, BLOCK), :] = dot(d_scores, keys[:hi], TN) * gq
        d_normed = dn_v[h] + dk_v[...] * gk + dv_v[...]
        dn_v[h] = d_normed
        return partial + row_sums(d_normed * wide)

    partial = lax.fori_loop(0, HEADS, backward, jnp.zeros((1, SEQ), jnp.float32))
    for b in range(ROWS):
        inner_v[pl.ds(b, 1), :] = partial[:, b * LANES : (b + 1) * LANES]
    inner_v[ROWS:8] = jnp.zeros((8 - ROWS, LANES), jnp.float32)
    shares_in = [remote(inner_v, inners_v.at[i], in_ss.at[i], in_rs.at[i], s, lax.rem(t + i, GROUP)) for i in range(1, GROUP)]
    for c in shares_in:
        c.start()
    for c in shares_in:
        c.wait_recv()
    inner = inner_v[...]
    for i in range(1, GROUP):
        inner = inner + inners_v[i]
    f = f_v[...]
    spread_columns(f * f * f * inner[0:ROWS] / DW, cb_v)

    def rows_of(c):
        return pl.ds(pl.multiple_of(c * CHUNK, CHUNK), CHUNK)

    def make(c):
        rows = rows_of(c)
        for h in range(HEADS):
            value = (g_v[h, rows, :].astype(jnp.float32) + fb_v[rows, :] * dn_v[h, rows, :]
                     - x_v[h, rows, :].astype(jnp.float32) * cb_v[rows, :])
            dx_v[rows, h * HDIM : (h + 1) * HDIM] = value.astype(jnp.bfloat16)

    def plain(c):
        return remote(dx_v.at[rows_of(c)], out_ref.at[rows_of(c)], dx_ss.at[c], dx_rs.at[c], section(-1), t)

    def leg(c, by):
        return remote(dx_v.at[rows_of(c)], relay_v.at[rows_of(c)], dx_ss.at[c], rel_rs.at[c], section(by), t)

    def onward(c, by):
        return remote(relay_v.at[rows_of(c)], out_ref.at[rows_of(c)], fwd_ss.at[c], dx_rs.at[c], section(by), t)

    half = CHUNKS // 2

    def loop(start, stop, body):
        def step(c, carry):
            body(c)
            return carry

        lax.fori_loop(start, stop, step, 0)

    @pl.when(jnp.logical_not(first))
    def _():
        def send(c):
            make(c)
            plain(c).start()

        loop(0, CHUNKS, send)

    @pl.when(first)
    def _():
        def send(c):
            make(c)
            leg(c, -PLANES).start()
            make(c + half)
            leg(c + half, PLANES - 1).start()

        def forward_on(c):
            leg(c, -PLANES).wait_recv()
            onward(c, PLANES - 1).start()

        loop(0, half, send)
        loop(0, half, forward_on)
        loop(0, half, lambda c: onward(c, PLANES - 1).wait_send())

    @pl.when(last)
    def _():
        def forward_on(c):
            leg(c, PLANES - 1).wait_recv()
            onward(c, -PLANES).start()

        loop(half, CHUNKS, forward_on)
        loop(half, CHUNKS, lambda c: onward(c, -PLANES).wait_send())

    def finish(c):
        plain(c).wait()

    loop(0, CHUNKS, finish)
    for h in range(HEADS):
        pltpu.make_async_copy(lo_v.at[h], lo_ref.at[:, pl.ds(h * HDIM, HDIM)], lo_s.at[h]).wait()
    for c in stash + shares + shares_in + [extra]:
        c.wait_send()


def local(layer_input, grad_input, stashed, eviction, query_gain, key_gain):
    head_buffer = pltpu.VMEM((HEADS, SEQ, HDIM), jnp.bfloat16)
    column = pltpu.VMEM((SEQ, HDIM), jnp.float32)
    dma = pltpu.SemaphoreType.DMA
    anywhere, vmem = pl.BlockSpec(memory_space=pl.ANY), pl.BlockSpec(memory_space=pltpu.VMEM)
    shape = jax.ShapeDtypeStruct((SEQ, HEADS * HDIM), jnp.bfloat16)
    output, passed = pl.pallas_call(
        kernel,
        out_shape=(shape, shape),
        in_specs=[pl.BlockSpec(memory_space=pltpu.SMEM), anywhere, anywhere, anywhere, vmem, vmem],
        out_specs=(anywhere, anywhere),
        scratch_shapes=[head_buffer] * 7 + [
            pltpu.VMEM((HEADS, SEQ, HDIM), jnp.float32), column, column,
            pltpu.VMEM((SEQ, HEADS * HDIM), jnp.bfloat16), pltpu.VMEM((SEQ, HEADS * HDIM), jnp.bfloat16),
            pltpu.VMEM((16, LANES), jnp.float32), pltpu.VMEM((GROUP, 16, LANES), jnp.float32),
            pltpu.VMEM((8, LANES), jnp.float32), pltpu.VMEM((8, LANES), jnp.float32),
            pltpu.VMEM((8, LANES), jnp.float32), pltpu.VMEM((GROUP, 8, LANES), jnp.float32),
            pltpu.VMEM((ROWS, LANES), jnp.float32), column, column,
        ] + [dma((HEADS,))] * 7 + [dma((GROUP,)), dma((GROUP,)), dma, dma, dma((GROUP,)), dma((GROUP,))]
        + [dma((CHUNKS,))] * 4,
        compiler_params=pltpu.CompilerParams(collective_id=0, has_side_effects=True, vmem_limit_bytes=56 * 2**20),
        name="tick",
    )(eviction, layer_input[0], grad_input[0], stashed[0], query_gain, key_gain)
    return (output[None], passed[None])


def solution(mesh):
    placed = (
        P("section", None, "tensor"),
        P("section", None, "tensor"),
        P("section", None, None, "tensor"),
        P("section"),
        P("section", "tensor"),
        P("section", "tensor"),
    )
    return jax.shard_map(
        local,
        mesh=mesh,
        in_specs=placed,
        out_specs=(P("section", None, "tensor"), P("section", None, "tensor")),
        check_vma=False,
    )
```

```python
import functools
import math

import jax
import jax.numpy as jnp
from jax import lax
from jax.experimental import pallas as pl
from jax.experimental.pallas import tpu as pltpu
from jax.sharding import PartitionSpec as P

MESH = pl.DeviceIdType.MESH
HDIM = 128
SEQ = 512
DW = 6144
SECTIONS = 48
PLANES = 12
GROUP = 16
HEADS = 3
BLOCK = 128
LANES = 128
ROWS = SEQ // LANES
CHUNK = 64
CHUNKS = SEQ // CHUNK
EPSILON = 1e-05
SCALE = 1.0 / math.sqrt(HDIM)
EXPONENT = SCALE * math.log2(math.e)
NT = (((1,), (1,)), ((), ()))
TN = (((0,), (0,)), ((), ()))
NN = (((1,), (0,)), ((), ()))


def dot(a, b, dims):
    return lax.dot_general(a, b, dims, preferred_element_type=jnp.float32)


def row_sums(values):
    high = values.astype(jnp.bfloat16)
    low = (values - high.astype(jnp.float32)).astype(jnp.bfloat16)
    ones = jnp.ones((8, values.shape[-1]), jnp.bfloat16)
    return (dot(ones, high, NT) + dot(ones, low, NT))[0:1]


def spread_columns(lane_rows, out_ref):
    for b in range(ROWS):
        block = jnp.broadcast_to(lane_rows[b : b + 1], (LANES, LANES))
        out_ref[pl.ds(b * LANES, LANES), :] = block.T


def block_weights(keys, queries, lo, hi):
    scores = dot(keys[:hi], queries[lo:hi], NT)
    width = hi - lo
    tail = scores[lo:]
    u = lax.broadcasted_iota(jnp.int32, (width, width), 0)
    t = lax.broadcasted_iota(jnp.int32, (width, width), 1)
    tail = jnp.where(u <= t, tail, -1e30)
    scores = tail if lo == 0 else jnp.concatenate([scores[:lo], tail], axis=0)
    top = jnp.max(scores, axis=0, keepdims=True)
    exponent = jnp.exp2((scores - top) * EXPONENT)
    return exponent * (1.0 / jnp.sum(exponent, axis=0, keepdims=True))


def kernel(
    ev_ref, li_ref, g_ref, st_ref, gq_ref, gk_ref,
    lo_ref, a_ref, x_ref, c_ref,
    ev_v, gq_v, gk_v, li_v, g_v, own_v, away_v, got_v, x_v, a_v, lo_v, dn_v, dk_v, dv_v, dx_v, relay_v,
    part_v, parts_v, extra_v, theirs_v, inner_v, inners_v, f_v, c_v, fb_v, cb_v,
    ready, small_s, li_s, g_s, own_s, away_s, lo_s,
    stash_ss, stash_rs, a_ss, a_rs, x_ss, x_rs, sq_ss, sq_rs, in_ss, in_rs, ex_ss, ex_rs, c_ss, c_rs,
    dx_ss, dx_rs, rel_rs, fwd_ss,
):
    s, t = lax.axis_index("section"), lax.axis_index("tensor")
    z = lax.rem(s, PLANES)
    first, last = z == 0, z == PLANES - 1
    inland = jnp.logical_not(first)

    def section(by):
        return lax.rem(s + (by + SECTIONS), SECTIONS)

    def remote(src, dst, ss, rs, to_s, to_t):
        return pltpu.make_async_remote_copy(
            src_ref=src, dst_ref=dst, send_sem=ss, recv_sem=rs,
            device_id={"section": to_s, "tensor": to_t}, device_id_type=MESH)

    barrier = pltpu.get_barrier_semaphore()

    def greet(to_s, to_t, semaphore=barrier):
        pl.semaphore_signal(semaphore, inc=1, device_id={"section": to_s, "tensor": to_t}, device_id_type=MESH)

    met = (SECTIONS // 2, -PLANES, PLANES)
    for by in met:
        greet(section(by), t)
    for by in range(1, GROUP):
        greet(s, lax.rem(t + by, GROUP))

    @pl.when(z >= 2)
    def _():
        greet(section(-1), t)

    @pl.when(jnp.logical_and(inland, jnp.logical_not(last)))
    def _():
        greet(section(1), t)

    def heads_in(src, dst, sems):
        return [pltpu.make_async_copy(src.at[:, pl.ds(h * HDIM, HDIM)], dst.at[h], sems.at[h]) for h in range(HEADS)]

    away_in = heads_in(st_ref.at[1], away_v, away_s)
    li_in = heads_in(li_ref, li_v, li_s)
    own_in = heads_in(st_ref.at[0], own_v, own_s)
    g_in = heads_in(g_ref, g_v, g_s)
    small_in = [
        pltpu.make_async_copy(ev_ref, ev_v, small_s.at[0]),
        pltpu.make_async_copy(gq_ref, gq_v, small_s.at[1]),
        pltpu.make_async_copy(gk_ref, gk_v, small_s.at[2]),
    ]
    for c in away_in + li_in + own_in + small_in + g_in:
        c.start()

    near = len(met) + GROUP - 1
    away_in[0].wait()
    pl.semaphore_wait(barrier, jnp.where(first, near, near + 2))

    @pl.when(first)
    def _():
        greet(section(1), t)
        greet(section(PLANES - 1), t)

    @pl.when(last)
    def _():
        greet(section(1 - PLANES), t, ready)

    def stash(h):
        return remote(away_v.at[h], got_v.at[h], stash_ss.at[h], stash_rs.at[h], section(SECTIONS // 2), t)

    stash(0).start()

    def squares(ref, slot):
        total = jnp.zeros((1, SEQ), jnp.float32)
        for h in range(HEADS):
            wide = ref[h].astype(jnp.float32)
            total = total + row_sums(wide * wide)
        for b in range(ROWS):
            part_v[pl.ds(slot * ROWS + b, 1), :] = total[:, b * LANES : (b + 1) * LANES]

    for c in away_in[1:]:
        c.wait()
    squares(away_v, 2)
    for c in li_in:
        c.wait()
    squares(li_v, 0)
    for c in own_in:
        c.wait()
    squares(own_v, 1)
    part_v[12:16] = jnp.zeros((4, LANES), jnp.float32)

    shares = [remote(part_v, parts_v.at[i], sq_ss.at[i], sq_rs.at[i], s, lax.rem(t + i, GROUP)) for i in range(1, GROUP)]
    for c in shares:
        c.start()
    stash(1).start()
    for c in small_in + g_in:
        c.wait()
    for c in shares:
        c.wait_recv()
    totals = part_v[...]
    for i in range(1, GROUP):
        totals = totals + parts_v[i]
    extra_v[...] = totals[8:16]
    extra = remote(extra_v, theirs_v, ex_ss, ex_rs, section(SECTIONS // 2), t)
    extra.start()
    stash(2).start()

    def factor_of(total):
        return lax.rsqrt(total / DW + EPSILON)

    spread_columns(factor_of(totals[0:ROWS]), fb_v)

    def forward(h, carry):
        cols = pl.ds(pl.multiple_of(h * HDIM, HDIM), HDIM)
        wide = li_v[h].astype(jnp.float32)
        normed = wide * fb_v[...]
        queries = (normed * gq_v[:, cols]).astype(jnp.bfloat16)
        keys = (normed * gk_v[:, cols]).astype(jnp.bfloat16)
        values = normed.astype(jnp.bfloat16)
        for lo in range(0, SEQ, BLOCK):
            hi = lo + BLOCK
            weights = block_weights(keys, queries, lo, hi).astype(jnp.bfloat16)
            mixed = dot(weights, values[:hi], TN)
            lo_v[h, pl.ds(lo, BLOCK), :] = (wide[lo:hi] + mixed).astype(jnp.bfloat16)
        pltpu.make_async_copy(lo_v.at[h], lo_ref.at[:, cols], lo_s.at[h]).start()
        return carry

    lax.fori_loop(0, HEADS, forward, 0)

    extra.wait_recv()
    evicted = jnp.full((ROWS, LANES), ev_v[0], jnp.int32) == 1
    f_v[...] = factor_of(jnp.where(evicted, theirs_v[0:ROWS], totals[4:8]))
    spread_columns(f_v[...], fb_v)
    picked = jnp.full((SEQ, HDIM), ev_v[0], jnp.int32) == 1

    def send_x(h):
        return remote(x_v.at[h], x_ref.at[h], x_ss.at[h], x_rs.at[h], section(-1), t)

    def send_a(h):
        return remote(a_v.at[h], a_ref.at[h], a_ss.at[h], a_rs.at[h], section(-1), t)

    def backward(h, partial):
        cols = pl.ds(pl.multiple_of(h * HDIM, HDIM), HDIM)
        stash(h).wait_recv()
        wide = jnp.where(picked, got_v[h].astype(jnp.float32), own_v[h].astype(jnp.float32))
        x_v[h] = wide.astype(jnp.bfloat16)

        @pl.when(inland)
        def _():
            send_x(h).start()

        normed = wide * fb_v[...]
        gq, gk = gq_v[:, cols], gk_v[:, cols]
        queries = (normed * gq).astype(jnp.bfloat16)
        keys = (normed * gk).astype(jnp.bfloat16)
        values = normed.astype(jnp.bfloat16)
        grads = g_v[h]
        for lo in range(SEQ - BLOCK, -1, -BLOCK):
            hi = lo + BLOCK
            weights = block_weights(keys, queries, lo, hi)
            d_weights = dot(values[:hi], grads[lo:hi], NT)
            delta = jnp.sum(weights * d_weights, axis=0, keepdims=True)
            d_scores = (weights * (d_weights - delta) * SCALE).astype(jnp.bfloat16)
            d_keys = dot(d_scores, queries[lo:hi], NN)
            d_values = dot(weights.astype(jnp.bfloat16), grads[lo:hi], NN)
            if hi == SEQ:
                dk_v[...] = d_keys
                dv_v[...] = d_values
            else:
                dk_v[0:hi] += d_keys
                dv_v[0:hi] += d_values
            dn_v[h, pl.ds(lo, BLOCK), :] = dot(d_scores, keys[:hi], TN) * gq
        d_normed = dn_v[h] + dk_v[...] * gk + dv_v[...]
        dn_v[h] = d_normed
        a_v[h] = (grads.astype(jnp.float32) + fb_v[...] * d_normed).astype(jnp.bfloat16)

        @pl.when(inland)
        def _():
            send_a(h).start()

        return partial + row_sums(d_normed * wide)

    partial = lax.fori_loop(0, HEADS, backward, jnp.zeros((1, SEQ), jnp.float32))
    for b in range(ROWS):
        inner_v[pl.ds(b, 1), :] = partial[:, b * LANES : (b + 1) * LANES]
    inner_v[ROWS:8] = jnp.zeros((8 - ROWS, LANES), jnp.float32)
    shares_in = [remote(inner_v, inners_v.at[i], in_ss.at[i], in_rs.at[i], s, lax.rem(t + i, GROUP)) for i in range(1, GROUP)]
    for c in shares_in:
        c.start()
    for c in shares_in:
        c.wait_recv()
    inner = inner_v[...]
    for i in range(1, GROUP):
        inner = inner + inners_v[i]
    f = f_v[...]
    scalars = f * f * f * inner[0:ROWS] / DW
    c_v[0:ROWS] = scalars
    c_v[ROWS:8] = jnp.zeros((8 - ROWS, LANES), jnp.float32)
    send_c = remote(c_v, c_ref, c_ss, c_rs, section(-1), t)

    @pl.when(inland)
    def _():
        send_c.start()

    def part(ref, c):
        return ref.at[:, pl.ds(pl.multiple_of(c * CHUNK, CHUNK), CHUNK)]

    def make(c):
        rows = pl.ds(pl.multiple_of(c * CHUNK, CHUNK), CHUNK)
        for h in range(HEADS):
            value = (g_v[h, rows, :].astype(jnp.float32) + fb_v[rows, :] * dn_v[h, rows, :]
                     - x_v[h, rows, :].astype(jnp.float32) * cb_v[rows, :])
            dx_v[h, rows, :] = value.astype(jnp.bfloat16)

    def leg(c, by):
        return remote(part(dx_v, c), part(relay_v, c), dx_ss.at[c], rel_rs.at[c], section(by), t)

    def onward(c, by):
        return remote(part(relay_v, c), part(a_ref, c), fwd_ss.at[c], dx_rs.at[c], section(by), t)

    half = CHUNKS // 2

    def loop(start, stop, body):
        def step(c, carry):
            body(c)
            return carry

        lax.fori_loop(start, stop, step, 0)

    @pl.when(first)
    def _():
        spread_columns(scalars, cb_v)
        pl.semaphore_wait(ready, 1)

        def send(c):
            make(c)
            leg(c, -PLANES).start()
            make(c + half)
            leg(c + half, PLANES - 1).start()

        def forward_on(c):
            leg(c, -PLANES).wait_recv()
            onward(c, PLANES - 1).start()

        loop(0, half, send)
        loop(0, half, forward_on)
        loop(0, half, lambda c: onward(c, PLANES - 1).wait_send())
        loop(0, CHUNKS, lambda c: leg(c, -PLANES).wait_send())

    @pl.when(last)
    def _():
        def forward_on(c):
            leg(c, PLANES - 1).wait_recv()
            onward(c, -PLANES).start()

        loop(half, CHUNKS, forward_on)
        loop(half, CHUNKS, lambda c: onward(c, -PLANES).wait_send())
        loop(0, CHUNKS, lambda c: onward(c, -PLANES).wait_recv())

    @pl.when(inland)
    def _():
        for h in range(HEADS):
            send_x(h).wait_send()
            send_a(h).wait_send()
        send_c.wait_send()

    for h in range(HEADS):
        pltpu.make_async_copy(lo_v.at[h], lo_ref.at[:, pl.ds(h * HDIM, HDIM)], lo_s.at[h]).wait()
        stash(h).wait_send()
    for c in shares + shares_in + [extra]:
        c.wait_send()

    @pl.when(jnp.logical_not(last))
    def _():
        for h in range(HEADS):
            send_x(h).wait_recv()
            send_a(h).wait_recv()
        send_c.wait_recv()


def finish(lo_ref, a_ref, x_ref, c_ref, out_ref, grad_ref, cb_v):
    last = lax.rem(lax.axis_index("section"), PLANES) == PLANES - 1
    out_ref[...] = lo_ref[...]

    @pl.when(last)
    def _():
        for h in range(HEADS):
            grad_ref[:, h * HDIM : (h + 1) * HDIM] = a_ref[h]

    @pl.when(jnp.logical_not(last))
    def _():
        spread_columns(c_ref[...], cb_v)
        for h in range(HEADS):
            value = a_ref[h].astype(jnp.float32) - x_ref[h].astype(jnp.float32) * cb_v[...]
            grad_ref[:, h * HDIM : (h + 1) * HDIM] = value.astype(jnp.bfloat16)


def local(layer_input, grad_input, stashed, eviction, query_gain, key_gain):
    head_buffer = pltpu.VMEM((HEADS, SEQ, HDIM), jnp.bfloat16)
    column = pltpu.VMEM((SEQ, HDIM), jnp.float32)
    gain = pltpu.VMEM((1, HEADS * HDIM), jnp.float32)
    tile = pltpu.VMEM((8, LANES), jnp.float32)
    dma = pltpu.SemaphoreType.DMA
    anywhere, vmem = pl.BlockSpec(memory_space=pl.ANY), pl.BlockSpec(memory_space=pltpu.VMEM)
    flat = jax.ShapeDtypeStruct((SEQ, HEADS * HDIM), jnp.bfloat16)
    split = jax.ShapeDtypeStruct((HEADS, SEQ, HDIM), jnp.bfloat16)
    lo, a, x, c = pl.pallas_call(
        kernel,
        out_shape=(flat, split, split, jax.ShapeDtypeStruct((8, LANES), jnp.float32)),
        in_specs=[anywhere] * 6,
        out_specs=(anywhere,) * 4,
        scratch_shapes=[pltpu.SMEM((1,), jnp.int32), gain, gain] + [head_buffer] * 8 + [
            pltpu.VMEM((HEADS, SEQ, HDIM), jnp.float32), column, column, head_buffer, head_buffer,
            pltpu.VMEM((16, LANES), jnp.float32), pltpu.VMEM((GROUP, 16, LANES), jnp.float32),
            tile, tile, tile, pltpu.VMEM((GROUP, 8, LANES), jnp.float32),
            pltpu.VMEM((ROWS, LANES), jnp.float32), tile, column, column, pltpu.SemaphoreType.REGULAR,
        ] + [dma((HEADS,))] * 12 + [dma((GROUP,))] * 4 + [dma] * 4 + [dma((CHUNKS,))] * 4,
        compiler_params=pltpu.CompilerParams(collective_id=0, has_side_effects=True, vmem_limit_bytes=56 * 2**20),
        name="tick",
    )(eviction, layer_input[0], grad_input[0], stashed[0], query_gain, key_gain)
    output, passed = pl.pallas_call(
        finish,
        out_shape=(flat, flat),
        in_specs=[vmem] * 4,
        out_specs=(vmem, vmem),
        scratch_shapes=[column],
        name="finish",
    )(lo, a, x, c)
    return (output[None], passed[None])


def solution(mesh):
    placed = (
        P("section", None, "tensor"),
        P("section", None, "tensor"),
        P("section", None, None, "tensor"),
        P("section"),
        P("section", "tensor"),
        P("section", "tensor"),
    )
    return jax.shard_map(
        local,
        mesh=mesh,
        in_specs=placed,
        out_specs=(P("section", None, "tensor"), P("section", None, "tensor")),
        check_vma=False,
    )
```

```python
import functools
import math

import jax
import jax.numpy as jnp
from jax import lax
from jax.experimental import pallas as pl
from jax.experimental.pallas import tpu as pltpu
from jax.sharding import PartitionSpec as P

MESH = pl.DeviceIdType.MESH
HDIM = 128
SEQ = 512
DW = 6144
SECTIONS = 48
PLANES = 12
GROUP = 16
HEADS = 3
BLOCK = 128
LANES = 128
ROWS = SEQ // LANES
CHUNK = 64
HALF = SEQ // 2
CHUNKS = HALF // CHUNK
EPSILON = 1e-05
SCALE = 1.0 / math.sqrt(HDIM)
EXPONENT = SCALE * math.log2(math.e)
NT = (((1,), (1,)), ((), ()))
TN = (((0,), (0,)), ((), ()))
NN = (((1,), (0,)), ((), ()))


def dot(a, b, dims):
    return lax.dot_general(a, b, dims, preferred_element_type=jnp.float32)


def row_sums(values):
    high = values.astype(jnp.bfloat16)
    low = (values - high.astype(jnp.float32)).astype(jnp.bfloat16)
    ones = jnp.ones((8, values.shape[-1]), jnp.bfloat16)
    return (dot(ones, high, NT) + dot(ones, low, NT))[0:1]


def spread_columns(row, out_ref):
    for lo in range(0, row.shape[1], LANES):
        block = jnp.broadcast_to(row[:, lo : lo + LANES], (LANES, LANES))
        out_ref[pl.ds(lo, LANES), :] = block.T


def one_row(rows):
    return jnp.concatenate([rows[b : b + 1] for b in range(ROWS)], axis=1)


def block_weights(keys, queries, lo, hi):
    scores = dot(keys[:hi], queries[lo:hi], NT)
    width = hi - lo
    tail = scores[lo:]
    u = lax.broadcasted_iota(jnp.int32, (width, width), 0)
    t = lax.broadcasted_iota(jnp.int32, (width, width), 1)
    tail = jnp.where(u <= t, tail, -1e30)
    scores = tail if lo == 0 else jnp.concatenate([scores[:lo], tail], axis=0)
    top = jnp.max(scores, axis=0, keepdims=True)
    exponent = jnp.exp2((scores - top) * EXPONENT)
    return exponent * (1.0 / jnp.sum(exponent, axis=0, keepdims=True))


def kernel(
    ev_ref, li_ref, g_ref, st_ref, gq_ref, gk_ref,
    lo_ref, a_ref, x_ref, c_ref,
    gq_v, gk_v, li_v, g_v, own_v, away_v, got_v, x_v, a_v, lo_v, dq_v, dk_v, dv_v, dx_v, hop_v, rx_v, ra_v, rc_v,
    part_v, parts_v, extra_v, theirs_v, inner_v, fb_v, cb_v,
    ready, opened, small_s, li_s, g_s, own_s, away_s, lo_s,
    stash_ss, stash_rs, a_ss, a_rs, x_ss, x_rs, wa_rs, wx_rs, sq_ss, sq_rs, c_ss, c_rs, wc_rs, ex_ss, ex_rs,
    wa_ss, wx_ss, wc_ss, dx_ss, hop_ss, hop_rs, dx_rs,
):
    s, t = lax.axis_index("section"), lax.axis_index("tensor")
    z = lax.rem(s, PLANES)
    first, last = z == 0, z == PLANES - 1
    inland = jnp.logical_not(first)

    def section(by):
        return lax.rem(s + (by + SECTIONS), SECTIONS)

    def remote(src, dst, ss, rs, to_s, to_t):
        return pltpu.make_async_remote_copy(
            src_ref=src, dst_ref=dst, send_sem=ss, recv_sem=rs,
            device_id={"section": to_s, "tensor": to_t}, device_id_type=MESH)

    barrier = pltpu.get_barrier_semaphore()

    def greet(to_s, to_t, semaphore=barrier):
        pl.semaphore_signal(semaphore, inc=1, device_id={"section": to_s, "tensor": to_t}, device_id_type=MESH)

    second, porter = z == 1, z >= PLANES - 2
    outer = z == PLANES - 2
    greet(section(SECTIONS // 2), t)
    for by in range(1, GROUP):
        greet(s, lax.rem(t + by, GROUP))

    def greet_plane(by, semaphore=barrier):
        for to_t in range(GROUP):
            greet(section(by), to_t, semaphore)

    @pl.when(jnp.logical_and(inland, jnp.logical_not(last)))
    def _():
        greet_plane(1)

    @pl.when(second)
    def _():
        greet_plane(-1)

    @pl.when(first)
    def _():
        greet_plane(PLANES - 1)
        greet_plane(PLANES - 2)

    @pl.when(porter)
    def _():
        greet(section(PLANES), t)

    @pl.when(last)
    def _():
        greet(section(-1), t)

    def heads_in(src, dst, sems):
        return [pltpu.make_async_copy(src.at[:, pl.ds(h * HDIM, HDIM)], dst.at[h], sems.at[h]) for h in range(HEADS)]

    away_in = heads_in(st_ref.at[1], away_v, away_s)
    li_in = heads_in(li_ref, li_v, li_s)
    own_in = heads_in(st_ref.at[0], own_v, own_s)
    g_in = heads_in(g_ref, g_v, g_s)
    small_in = [
        pltpu.make_async_copy(gq_ref, gq_v, small_s.at[1]),
        pltpu.make_async_copy(gk_ref, gk_v, small_s.at[2]),
    ]
    for c in away_in + li_in + own_in + small_in + g_in:
        c.start()

    def count(condition):
        return condition.astype(jnp.int32)

    @pl.when(porter)
    def _():
        pl.semaphore_wait(barrier, 3 * GROUP + 1 + count(outer))
        for to_t in range(GROUP):
            greet(lax.rem(s - z + SECTIONS, SECTIONS), to_t, ready)

    def squares(ref, slot):
        total = jnp.zeros((1, SEQ), jnp.float32)
        for h in range(HEADS):
            wide = ref[h].astype(jnp.float32)
            total = total + row_sums(wide * wide)
        for b in range(ROWS):
            part_v[pl.ds(slot * ROWS + b, 1), :] = total[:, b * LANES : (b + 1) * LANES]

    for c in away_in:
        c.wait()
    squares(away_v, 2)
    for c in li_in:
        c.wait()
    squares(li_v, 0)
    for c in own_in:
        c.wait()
    squares(own_v, 1)
    part_v[12:16] = jnp.zeros((4, LANES), jnp.float32)

    @pl.when(jnp.logical_not(porter))
    def _():
        pl.semaphore_wait(barrier, GROUP + GROUP * count(z != 1))

    @pl.when(first)
    def _():
        greet_plane(1, opened)

    def stash(h):
        return remote(away_v.at[h], got_v.at[h], stash_ss.at[h], stash_rs.at[h], section(SECTIONS // 2), t)

    shares = [remote(part_v, parts_v.at[i], sq_ss.at[i], sq_rs.at[i], s, lax.rem(t + i, GROUP)) for i in range(1, GROUP)]
    for c in shares:
        c.start()
    stash(0).start()
    for c in small_in + g_in:
        c.wait()
    for c in shares:
        c.wait_recv()
    totals = part_v[...]
    for i in range(1, GROUP):
        totals = totals + parts_v[i]
    extra_v[...] = totals[8:16]
    extra = remote(extra_v, theirs_v, ex_ss, ex_rs, section(SECTIONS // 2), t)
    extra.start()
    stash(1).start()
    stash(2).start()

    def factor_of(total):
        return lax.rsqrt(total / DW + EPSILON)

    spread_columns(factor_of(one_row(totals[0:ROWS])), fb_v)

    def forward(h, carry):
        cols = pl.ds(pl.multiple_of(h * HDIM, HDIM), HDIM)
        wide = li_v[h].astype(jnp.float32)
        normed = wide * fb_v[...]
        queries = (normed * gq_v[:, cols]).astype(jnp.bfloat16)
        keys = (normed * gk_v[:, cols]).astype(jnp.bfloat16)
        values = normed.astype(jnp.bfloat16)
        for lo in range(0, SEQ, BLOCK):
            hi = lo + BLOCK
            weights = block_weights(keys, queries, lo, hi).astype(jnp.bfloat16)
            mixed = dot(weights, values[:hi], TN)
            lo_v[h, pl.ds(lo, BLOCK), :] = (wide[lo:hi] + mixed).astype(jnp.bfloat16)
        pltpu.make_async_copy(lo_v.at[h], lo_ref.at[h], lo_s.at[h]).start()
        return carry

    lax.fori_loop(0, HEADS, forward, 0)

    picked = jnp.full((SEQ, HDIM), ev_ref[0], jnp.int32) == 1

    def send_x(h):
        return remote(x_v.at[h], x_ref.at[h], x_ss.at[h], x_rs.at[h], section(-1), t)

    def send_a(h):
        return remote(a_v.at[h], a_ref.at[h], a_ss.at[h], a_rs.at[h], section(-1), t)

    def wrap_x(h, k):
        rows = pl.ds(k * HALF, HALF)
        return remote(x_v.at[h, rows], rx_v.at[h], wx_ss.at[k, h], wx_rs.at[h], section(PLANES - 1 - k), t)

    def wrap_a(h, k):
        rows = pl.ds(k * HALF, HALF)
        return remote(a_v.at[h, rows], ra_v.at[h], wa_ss.at[k, h], wa_rs.at[h], section(PLANES - 1 - k), t)

    def send_c(i):
        return remote(inner_v, c_ref.at[i], c_ss.at[i], c_rs.at[i], section(-1), lax.rem(t + i, GROUP))

    def wrap_c(i, k):
        tokens = pl.ds(k * HALF, HALF)
        return remote(inner_v.at[:, tokens], rc_v.at[i], wc_ss.at[k, i], wc_rs.at[i], section(PLANES - 1 - k), lax.rem(t + i, GROUP))

    def pass_on(whole, halves, h):
        @pl.when(inland)
        def _():
            whole(h).start()

        @pl.when(first)
        def _():
            halves(h, 0).start()
            halves(h, 1).start()

    def choose(h):
        stash(h).wait_recv()
        wide = jnp.where(picked, got_v[h].astype(jnp.float32), own_v[h].astype(jnp.float32))
        x_v[h] = wide.astype(jnp.bfloat16)
        pass_on(send_x, wrap_x, h)

    @pl.when(second)
    def _():
        pl.semaphore_wait(opened, GROUP)

    @pl.when(first)
    def _():
        pl.semaphore_wait(ready, 2 * GROUP)

    choose(0)
    extra.wait_recv()
    evicted = jnp.full((1, SEQ), ev_ref[0], jnp.int32) == 1
    f = factor_of(jnp.where(evicted, one_row(theirs_v[0:ROWS]), one_row(totals[4:8])))
    spread_columns(f, fb_v)

    def backward(h, partial):
        cols = pl.ds(pl.multiple_of(h * HDIM, HDIM), HDIM)
        wide = x_v[h].astype(jnp.float32)
        normed = wide * fb_v[...]
        gq, gk = gq_v[:, cols], gk_v[:, cols]
        queries = (normed * gq).astype(jnp.bfloat16)
        keys = (normed * gk).astype(jnp.bfloat16)
        values = normed.astype(jnp.bfloat16)
        grads = g_v[h]
        for lo in range(SEQ - BLOCK, -1, -BLOCK):
            hi = lo + BLOCK
            weights = block_weights(keys, queries, lo, hi)
            d_weights = dot(values[:hi], grads[lo:hi], NT)
            delta = jnp.sum(weights * d_weights, axis=0, keepdims=True)
            d_scores = (weights * (d_weights - delta) * SCALE).astype(jnp.bfloat16)
            d_keys = dot(d_scores, queries[lo:hi], NN)
            d_values = dot(weights.astype(jnp.bfloat16), grads[lo:hi], NN)
            if hi == SEQ:
                dk_v[...] = d_keys
                dv_v[...] = d_values
            else:
                dk_v[0:hi] += d_keys
                dv_v[0:hi] += d_values
            dq_v[pl.ds(lo, BLOCK), :] = dot(d_scores, keys[:hi], TN) * gq
        d_normed = dq_v[...] + dk_v[...] * gk + dv_v[...]
        a_v[h] = (grads.astype(jnp.float32) + fb_v[...] * d_normed).astype(jnp.bfloat16)

        @pl.when(h < HEADS - 1)
        def _():
            pass_on(send_a, wrap_a, h)
            choose(h + 1)

        return partial + row_sums(d_normed * wide)

    partial = lax.fori_loop(0, HEADS, backward, jnp.zeros((1, SEQ), jnp.float32))
    inner_v[...] = partial * (f * f * f * (1.0 / DW))

    @pl.when(inland)
    def _():
        for i in range(GROUP):
            send_c(i).start()

    @pl.when(first)
    def _():
        for i in range(GROUP):
            wrap_c(i, 0).start()
            wrap_c(i, 1).start()

    pass_on(send_a, wrap_a, HEADS - 1)

    def rows_at(c, base=0):
        return pl.ds(pl.multiple_of(base + c * CHUNK, CHUNK), CHUNK)

    def carry(c):
        return remote(dx_v.at[:, rows_at(c)], a_ref.at[:, rows_at(c)], dx_ss.at[c], dx_rs.at[c], section(-PLANES), t)

    def leg(c):
        return remote(dx_v.at[:, rows_at(c)], hop_v.at[:, rows_at(c)], dx_ss.at[c], hop_rs.at[c], section(-PLANES), t)

    def land(c):
        return remote(hop_v.at[:, rows_at(c)], a_ref.at[:, rows_at(c, HALF)], hop_ss.at[c], dx_rs.at[CHUNKS + c], section(1), t)

    @pl.when(porter)
    def _():
        for i in range(GROUP):
            wrap_c(i, 0).wait_recv()
        total = rc_v[0]
        for i in range(1, GROUP):
            total = total + rc_v[i]
        spread_columns(total, cb_v)
        for h in range(HEADS):
            wrap_x(h, 0).wait_recv()
            wrap_a(h, 0).wait_recv()

        def step(c, carried):
            rows = rows_at(c)
            for h in range(HEADS):
                value = ra_v[h, rows, :].astype(jnp.float32) - rx_v[h, rows, :].astype(jnp.float32) * cb_v[rows, :]
                dx_v[h, rows, :] = value.astype(jnp.bfloat16)

            @pl.when(last)
            def _():
                carry(c).start()

            @pl.when(outer)
            def _():
                leg(c).start()

            return carried

        lax.fori_loop(0, CHUNKS, step, 0)

    @pl.when(outer)
    def _():
        for c in range(CHUNKS):
            leg(c).wait_recv()
            land(c).start()
        for c in range(CHUNKS):
            leg(c).wait_send()
            land(c).wait_send()

    @pl.when(last)
    def _():
        for c in range(CHUNKS):
            carry(c).wait_send()

    @pl.when(last)
    def _():
        for c in range(2 * CHUNKS):
            rows = pl.ds(c * CHUNK, CHUNK)
            remote(a_ref.at[:, rows], a_ref.at[:, rows], dx_ss.at[0], dx_rs.at[c], section(-PLANES), t).wait_recv()

    @pl.when(first)
    def _():
        for k in range(2):
            for h in range(HEADS):
                wrap_x(h, k).wait_send()
                wrap_a(h, k).wait_send()
            for i in range(GROUP):
                wrap_c(i, k).wait_send()

    @pl.when(inland)
    def _():
        for h in range(HEADS):
            send_x(h).wait_send()
            send_a(h).wait_send()
        for i in range(GROUP):
            send_c(i).wait_send()

    for h in range(HEADS):
        stash(h).wait_send()
        pltpu.make_async_copy(lo_v.at[h], lo_ref.at[h], lo_s.at[h]).wait()
    for c in shares + [extra]:
        c.wait_send()

    @pl.when(jnp.logical_not(last))
    def _():
        for h in range(HEADS):
            send_x(h).wait_recv()
            send_a(h).wait_recv()
        for i in range(GROUP):
            send_c(i).wait_recv()


def finish(lo_ref, a_ref, x_ref, c_ref, out_ref, grad_ref, lo_v, a_v, x_v, c_v, grad_v, cb_v, in_s, out_s):
    last = lax.rem(lax.axis_index("section"), PLANES) == PLANES - 1

    def columns(ref, h):
        return ref.at[:, pl.ds(h * HDIM, HDIM)]

    scalars_in = pltpu.make_async_copy(c_ref, c_v, in_s.at[3 * HEADS])
    scalars_in.start()
    arrivals = [
        [pltpu.make_async_copy(src.at[h], dst.at[h], in_s.at[k * HEADS + h])
         for k, (src, dst) in enumerate(((lo_ref, lo_v), (a_ref, a_v), (x_ref, x_v)))]
        for h in range(HEADS)
    ]
    for copies in arrivals:
        for c in copies:
            c.start()
    scalars_in.wait()
    total = c_v[0]
    for i in range(1, GROUP):
        total = total + c_v[i]
    spread_columns(total, cb_v)
    leaving = []
    for h in range(HEADS):
        for c in arrivals[h]:
            c.wait()
        passed_on = pltpu.make_async_copy(lo_v.at[h], columns(out_ref, h), out_s.at[h])
        passed_on.start()
        leaving.append(passed_on)

        @pl.when(last)
        def _():
            grad_v[h] = a_v[h]

        @pl.when(jnp.logical_not(last))
        def _():
            value = a_v[h].astype(jnp.float32) - x_v[h].astype(jnp.float32) * cb_v[...]
            grad_v[h] = value.astype(jnp.bfloat16)

        made = pltpu.make_async_copy(grad_v.at[h], columns(grad_ref, h), out_s.at[HEADS + h])
        made.start()
        leaving.append(made)
    for c in leaving:
        c.wait()


def local(layer_input, grad_input, stashed, eviction, query_gain, key_gain):
    head_buffer = pltpu.VMEM((HEADS, SEQ, HDIM), jnp.bfloat16)
    half_buffer = pltpu.VMEM((HEADS, HALF, HDIM), jnp.bfloat16)
    column = pltpu.VMEM((SEQ, HDIM), jnp.float32)
    gain = pltpu.VMEM((1, HEADS * HDIM), jnp.float32)
    tile = pltpu.VMEM((8, LANES), jnp.float32)
    dma = pltpu.SemaphoreType.DMA
    anywhere = pl.BlockSpec(memory_space=pl.ANY)
    flat = jax.ShapeDtypeStruct((SEQ, HEADS * HDIM), jnp.bfloat16)
    split = jax.ShapeDtypeStruct((HEADS, SEQ, HDIM), jnp.bfloat16)
    lo, a, x, c = pl.pallas_call(
        kernel,
        out_shape=(split, split, split, jax.ShapeDtypeStruct((GROUP, 1, SEQ), jnp.float32)),
        in_specs=[pl.BlockSpec(memory_space=pltpu.SMEM)] + [anywhere] * 5,
        out_specs=(anywhere,) * 4,
        scratch_shapes=[gain, gain] + [head_buffer] * 8 + [column] * 3 + [half_buffer] * 4 + [
            pltpu.VMEM((GROUP, 1, HALF), jnp.float32),
            pltpu.VMEM((16, LANES), jnp.float32), pltpu.VMEM((GROUP, 16, LANES), jnp.float32),
            tile, tile, pltpu.VMEM((1, SEQ), jnp.float32), column, pltpu.VMEM((HALF, HDIM), jnp.float32),
            pltpu.SemaphoreType.REGULAR, pltpu.SemaphoreType.REGULAR,
        ] + [dma((HEADS,))] * 14 + [dma((GROUP,))] * 5 + [dma] * 2
        + [dma((2, HEADS)), dma((2, HEADS)), dma((2, GROUP)), dma((CHUNKS,)), dma((CHUNKS,)), dma((CHUNKS,)), dma((2 * CHUNKS,))],
        compiler_params=pltpu.CompilerParams(collective_id=0, has_side_effects=True, vmem_limit_bytes=60 * 2**20),
        name="tick",
    )(eviction, layer_input[0], grad_input[0], stashed[0], query_gain, key_gain)
    output, passed = pl.pallas_call(
        finish,
        out_shape=(flat, flat),
        in_specs=[anywhere] * 4,
        out_specs=(anywhere, anywhere),
        scratch_shapes=[head_buffer] * 3 + [
            pltpu.VMEM((GROUP, 1, SEQ), jnp.float32), head_buffer, column, dma((3 * HEADS + 1,)), dma((2 * HEADS,)),
        ],
        compiler_params=pltpu.CompilerParams(vmem_limit_bytes=60 * 2**20),
        name="finish",
    )(lo, a, x, c)
    return (output[None], passed[None])


def solution(mesh):
    placed = (
        P("section", None, "tensor"),
        P("section", None, "tensor"),
        P("section", None, None, "tensor"),
        P("section"),
        P("section", "tensor"),
        P("section", "tensor"),
    )
    return jax.shard_map(
        local,
        mesh=mesh,
        in_specs=placed,
        out_specs=(P("section", None, "tensor"), P("section", None, "tensor")),
        check_vma=False,
    )
```

```python
import functools
import math

import jax
import jax.numpy as jnp
from jax import lax
from jax.experimental import pallas as pl
from jax.experimental.pallas import tpu as pltpu
from jax.sharding import PartitionSpec as P

MESH = pl.DeviceIdType.MESH
HDIM = 128
SEQ = 512
DW = 6144
SECTIONS = 48
PLANES = 12
GROUP = 16
HEADS = 3
EARLY = HEADS - 1
BLOCK = 128
LANES = 128
ROWS = SEQ // LANES
CHUNK = 64
SHARES = ((0, 3), (3, 3), (6, 2))
WIDEST = 3 * CHUNK
CHUNKS = SEQ // CHUNK
EPSILON = 1e-05
SCALE = 1.0 / math.sqrt(HDIM)
EXPONENT = SCALE * math.log2(math.e)
NT = (((1,), (1,)), ((), ()))
TN = (((0,), (0,)), ((), ()))
NN = (((1,), (0,)), ((), ()))


def dot(a, b, dims):
    return lax.dot_general(a, b, dims, preferred_element_type=jnp.float32)


def row_sums(values):
    high = values.astype(jnp.bfloat16)
    low = (values - high.astype(jnp.float32)).astype(jnp.bfloat16)
    ones = jnp.ones((8, values.shape[-1]), jnp.bfloat16)
    return (dot(ones, high, NT) + dot(ones, low, NT))[0:1]


def spread_columns(row, out_ref):
    for lo in range(0, row.shape[1], LANES):
        block = jnp.broadcast_to(row[:, lo : lo + LANES], (LANES, LANES))
        out_ref[pl.ds(lo, LANES), :] = block.T


def one_row(rows):
    return jnp.concatenate([rows[b : b + 1] for b in range(ROWS)], axis=1)


def block_weights(keys, queries, lo, hi):
    scores = dot(keys[:hi], queries[lo:hi], NT)
    width = hi - lo
    tail = scores[lo:]
    u = lax.broadcasted_iota(jnp.int32, (width, width), 0)
    t = lax.broadcasted_iota(jnp.int32, (width, width), 1)
    tail = jnp.where(u <= t, tail, -1e30)
    scores = tail if lo == 0 else jnp.concatenate([scores[:lo], tail], axis=0)
    top = jnp.max(scores, axis=0, keepdims=True)
    exponent = jnp.exp2((scores - top) * EXPONENT)
    return exponent * (1.0 / jnp.sum(exponent, axis=0, keepdims=True))


def kernel(
    ev_ref, li_ref, g_ref, st_ref, gq_ref, gk_ref,
    lo_ref, a_ref, x_ref, c_ref,
    gq_v, gk_v, li_v, g_v, own_v, away_v, got_v, x_v, a_v, lo_v, dq_v, dk_v, dv_v, dx_v, hop_v, rx_v, ra_v, rc_v,
    part_v, parts_v, extra_v, theirs_v, inner_v, inners_v, c_v, fb_v, cb_v,
    ready, opened, small_s, li_s, g_s, own_s, away_s, lo_s,
    stash_ss, stash_rs, a_ss, a_rs, x_ss, x_rs, wa_rs, wx_rs, sq_ss, sq_rs, in_ss, in_rs, ex_ss, ex_rs, c_ss, c_rs, wc_rs,
    wa_ss, wx_ss, wc_ss, dx_ss, hop_ss, hop_rs, dx_rs,
):
    s, t = lax.axis_index("section"), lax.axis_index("tensor")
    z = lax.rem(s, PLANES)
    first, last = z == 0, z == PLANES - 1
    inland = jnp.logical_not(first)

    def section(by):
        return lax.rem(s + (by + SECTIONS), SECTIONS)

    def remote(src, dst, ss, rs, to_s, to_t):
        return pltpu.make_async_remote_copy(
            src_ref=src, dst_ref=dst, send_sem=ss, recv_sem=rs,
            device_id={"section": to_s, "tensor": to_t}, device_id_type=MESH)

    barrier = pltpu.get_barrier_semaphore()

    def greet(to_s, to_t, semaphore=barrier):
        pl.semaphore_signal(semaphore, inc=1, device_id={"section": to_s, "tensor": to_t}, device_id_type=MESH)

    second, porter = z == 1, z >= PLANES - len(SHARES)
    outer = jnp.logical_and(porter, jnp.logical_not(last))
    greet(section(SECTIONS // 2), t)
    for by in range(1, GROUP):
        greet(s, lax.rem(t + by, GROUP))

    @pl.when(jnp.logical_and(inland, jnp.logical_not(last)))
    def _():
        greet(section(1), t)

    @pl.when(second)
    def _():
        greet(section(-1), t)

    @pl.when(first)
    def _():
        for k in range(len(SHARES)):
            greet(section(PLANES - 1 - k), t)

    @pl.when(porter)
    def _():
        greet(section(PLANES), t)

    @pl.when(last)
    def _():
        for k in range(1, len(SHARES)):
            greet(section(-k), t)

    def heads_in(src, dst, sems):
        return [pltpu.make_async_copy(src.at[:, pl.ds(h * HDIM, HDIM)], dst.at[h], sems.at[h]) for h in range(HEADS)]

    away_in = heads_in(st_ref.at[1], away_v, away_s)
    li_in = heads_in(li_ref, li_v, li_s)
    own_in = heads_in(st_ref.at[0], own_v, own_s)
    g_in = heads_in(g_ref, g_v, g_s)
    small_in = [
        pltpu.make_async_copy(gq_ref, gq_v, small_s.at[1]),
        pltpu.make_async_copy(gk_ref, gk_v, small_s.at[2]),
    ]
    for c in away_in + li_in + own_in + small_in + g_in:
        c.start()

    def count(condition):
        return condition.astype(jnp.int32)

    @pl.when(porter)
    def _():
        pl.semaphore_wait(barrier, GROUP + 3 + count(outer))
        greet(lax.rem(s - z + SECTIONS, SECTIONS), t, ready)

    def squares(ref, slot):
        total = jnp.zeros((1, SEQ), jnp.float32)
        for h in range(HEADS):
            wide = ref[h].astype(jnp.float32)
            total = total + row_sums(wide * wide)
        for b in range(ROWS):
            part_v[pl.ds(slot * ROWS + b, 1), :] = total[:, b * LANES : (b + 1) * LANES]

    for c in away_in:
        c.wait()
    squares(away_v, 2)
    for c in li_in:
        c.wait()
    squares(li_v, 0)
    for c in own_in:
        c.wait()
    squares(own_v, 1)
    part_v[12:16] = jnp.zeros((4, LANES), jnp.float32)

    @pl.when(jnp.logical_not(porter))
    def _():
        pl.semaphore_wait(barrier, GROUP + count(z != 1))

    @pl.when(first)
    def _():
        greet(section(1), t, opened)

    def stash(h):
        return remote(away_v.at[h], got_v.at[h], stash_ss.at[h], stash_rs.at[h], section(SECTIONS // 2), t)

    shares = [remote(part_v, parts_v.at[i], sq_ss.at[i], sq_rs.at[i], s, lax.rem(t + i, GROUP)) for i in range(1, GROUP)]
    for c in shares:
        c.start()
    stash(0).start()
    for c in small_in + g_in:
        c.wait()
    for c in shares:
        c.wait_recv()
    totals = part_v[...]
    for i in range(1, GROUP):
        totals = totals + parts_v[i]
    extra_v[...] = totals[8:16]
    extra = remote(extra_v, theirs_v, ex_ss, ex_rs, section(SECTIONS // 2), t)
    extra.start()
    stash(1).start()
    stash(2).start()

    def factor_of(total):
        return lax.rsqrt(total / DW + EPSILON)

    spread_columns(factor_of(one_row(totals[0:ROWS])), fb_v)

    def forward(h, carry):
        cols = pl.ds(pl.multiple_of(h * HDIM, HDIM), HDIM)
        wide = li_v[h].astype(jnp.float32)
        normed = wide * fb_v[...]
        queries = (normed * gq_v[:, cols]).astype(jnp.bfloat16)
        keys = (normed * gk_v[:, cols]).astype(jnp.bfloat16)
        values = normed.astype(jnp.bfloat16)
        for lo in range(0, SEQ, BLOCK):
            hi = lo + BLOCK
            weights = block_weights(keys, queries, lo, hi).astype(jnp.bfloat16)
            mixed = dot(weights, values[:hi], TN)
            lo_v[h, pl.ds(lo, BLOCK), :] = (wide[lo:hi] + mixed).astype(jnp.bfloat16)
        pltpu.make_async_copy(lo_v.at[h], lo_ref.at[h], lo_s.at[h]).start()
        return carry

    lax.fori_loop(0, HEADS, forward, 0)

    picked = jnp.full((SEQ, HDIM), ev_ref[0], jnp.int32) == 1

    def send_x(h):
        return remote(x_v.at[h], x_ref.at[h], x_ss.at[h], x_rs.at[h], section(-1), t)

    def send_a(h):
        return remote(a_v.at[h], a_ref.at[h], a_ss.at[h], a_rs.at[h], section(-1), t)

    def wrap_x(h, k):
        start, count = SHARES[k]
        rows, held = pl.ds(start * CHUNK, count * CHUNK), pl.ds(0, count * CHUNK)
        return remote(x_v.at[h, rows], rx_v.at[h, held], wx_ss.at[k, h], wx_rs.at[h], section(PLANES - 1 - k), t)

    def wrap_a(h, k):
        start, count = SHARES[k]
        rows, held = pl.ds(start * CHUNK, count * CHUNK), pl.ds(0, count * CHUNK)
        return remote(a_v.at[h, rows], ra_v.at[h, held], wa_ss.at[k, h], wa_rs.at[h], section(PLANES - 1 - k), t)

    def share_in(i):
        return remote(inner_v, inners_v.at[i], in_ss.at[i], in_rs.at[i], s, lax.rem(t + i, GROUP))

    send_c = remote(c_v, c_ref, c_ss, c_rs, section(-1), t)

    def wrap_c(k):
        return remote(c_v, rc_v, wc_ss.at[k], wc_rs, section(PLANES - 1 - k), t)

    def pass_on(whole, halves, h):
        @pl.when(inland)
        def _():
            whole(h).start()

        @pl.when(first)
        def _():
            for k in range(len(SHARES)):
                halves(h, k).start()

    def choose(h):
        stash(h).wait_recv()
        wide = jnp.where(picked, got_v[h].astype(jnp.float32), own_v[h].astype(jnp.float32))
        x_v[h] = wide.astype(jnp.bfloat16)

        @pl.when(h < EARLY)
        def _():
            pass_on(send_x, wrap_x, h)

    @pl.when(second)
    def _():
        pl.semaphore_wait(opened, 1)

    @pl.when(first)
    def _():
        pl.semaphore_wait(ready, len(SHARES))

    choose(0)
    extra.wait_recv()
    evicted = jnp.full((1, SEQ), ev_ref[0], jnp.int32) == 1
    f = factor_of(jnp.where(evicted, one_row(theirs_v[0:ROWS]), one_row(totals[4:8])))
    spread_columns(f, fb_v)

    def backward(h, partial):
        cols = pl.ds(pl.multiple_of(h * HDIM, HDIM), HDIM)
        wide = x_v[h].astype(jnp.float32)
        normed = wide * fb_v[...]
        gq, gk = gq_v[:, cols], gk_v[:, cols]
        queries = (normed * gq).astype(jnp.bfloat16)
        keys = (normed * gk).astype(jnp.bfloat16)
        values = normed.astype(jnp.bfloat16)
        grads = g_v[h]
        for lo in range(SEQ - BLOCK, -1, -BLOCK):
            hi = lo + BLOCK
            weights = block_weights(keys, queries, lo, hi)
            d_weights = dot(values[:hi], grads[lo:hi], NT)
            delta = jnp.sum(weights * d_weights, axis=0, keepdims=True)
            d_scores = (weights * (d_weights - delta) * SCALE).astype(jnp.bfloat16)
            d_keys = dot(d_scores, queries[lo:hi], NN)
            d_values = dot(weights.astype(jnp.bfloat16), grads[lo:hi], NN)
            if hi == SEQ:
                dk_v[...] = d_keys
                dv_v[...] = d_values
            else:
                dk_v[0:hi] += d_keys
                dv_v[0:hi] += d_values
            dq_v[pl.ds(lo, BLOCK), :] = dot(d_scores, keys[:hi], TN) * gq
        d_normed = dq_v[...] + dk_v[...] * gk + dv_v[...]
        a32 = grads.astype(jnp.float32) + fb_v[...] * d_normed
        dq_v[...] = a32

        @pl.when(h < EARLY)
        def _():
            a_v[h] = a32.astype(jnp.bfloat16)
            pass_on(send_a, wrap_a, h)
            choose(h + 1)

        return partial + row_sums(d_normed * wide)

    partial = lax.fori_loop(0, HEADS, backward, jnp.zeros((1, SEQ), jnp.float32))
    inner_v[...] = partial * (f * f * f * (1.0 / DW))
    for i in range(1, GROUP):
        share_in(i).start()

    def rows_at(c):
        return pl.ds(c * CHUNK, CHUNK)

    def carry(c):
        return remote(dx_v.at[:, rows_at(c)], a_ref.at[:, rows_at(c)], dx_ss.at[c], dx_rs.at[c], section(-PLANES), t)

    def leg(c):
        return remote(dx_v.at[:, rows_at(c)], hop_v.at[:, rows_at(c)], dx_ss.at[c], hop_rs.at[c], section(-PLANES), t)

    def land(c, k):
        at = SHARES[k][0] + c
        return remote(hop_v.at[:, rows_at(c)], a_ref.at[:, rows_at(at)], hop_ss.at[c], dx_rs.at[at], section(k), t)

    @pl.when(porter)
    def _():
        wrap_c(0).wait_recv()
        spread_columns(rc_v[...], cb_v)
        for k, (start, chunks) in enumerate(SHARES):
            @pl.when(z == PLANES - 1 - k)
            def _():
                for h in range(EARLY):
                    wrap_x(h, k).wait_recv()
                for h in range(HEADS):
                    wrap_a(h, k).wait_recv()
                for c in range(chunks):
                    rows, tokens = rows_at(c), rows_at(start + c)
                    dx_v[EARLY, rows, :] = ra_v[EARLY, rows, :]
                    for h in range(EARLY):
                        value = ra_v[h, rows, :].astype(jnp.float32) - rx_v[h, rows, :].astype(jnp.float32) * cb_v[tokens, :]
                        dx_v[h, rows, :] = value.astype(jnp.bfloat16)
                    (leg(c) if k else carry(c)).start()

    for i in range(1, GROUP):
        share_in(i).wait_recv()
    scalars = inner_v[...]
    for i in range(1, GROUP):
        scalars = scalars + inners_v[i]
    c_v[...] = scalars

    @pl.when(inland)
    def _():
        send_c.start()

    @pl.when(first)
    def _():
        for k in range(len(SHARES)):
            wrap_c(k).start()

    spread_columns(scalars, cb_v)
    a_v[EARLY] = (dq_v[...] - x_v[EARLY].astype(jnp.float32) * cb_v[...]).astype(jnp.bfloat16)
    pass_on(send_a, wrap_a, EARLY)

    @pl.when(outer)
    def _():
        for k in range(1, len(SHARES)):
            @pl.when(z == PLANES - 1 - k)
            def _():
                for c in range(SHARES[k][1]):
                    leg(c).wait_recv()
                    land(c, k).start()
                for c in range(SHARES[k][1]):
                    leg(c).wait_send()
                    land(c, k).wait_send()

    @pl.when(last)
    def _():
        for c in range(SHARES[0][1]):
            carry(c).wait_send()

    @pl.when(last)
    def _():
        for c in range(CHUNKS):
            rows = pl.ds(c * CHUNK, CHUNK)
            remote(a_ref.at[:, rows], a_ref.at[:, rows], dx_ss.at[0], dx_rs.at[c], section(-PLANES), t).wait_recv()

    @pl.when(first)
    def _():
        for k in range(len(SHARES)):
            for h in range(EARLY):
                wrap_x(h, k).wait_send()
            for h in range(HEADS):
                wrap_a(h, k).wait_send()
            wrap_c(k).wait_send()

    @pl.when(inland)
    def _():
        for h in range(EARLY):
            send_x(h).wait_send()
        for h in range(HEADS):
            send_a(h).wait_send()
        send_c.wait_send()

    for h in range(HEADS):
        stash(h).wait_send()
        pltpu.make_async_copy(lo_v.at[h], lo_ref.at[h], lo_s.at[h]).wait()
    for c in shares + [share_in(i) for i in range(1, GROUP)] + [extra]:
        c.wait_send()

    @pl.when(jnp.logical_not(last))
    def _():
        for h in range(EARLY):
            send_x(h).wait_recv()
        for h in range(HEADS):
            send_a(h).wait_recv()
        send_c.wait_recv()


def finish(lo_ref, a_ref, x_ref, c_ref, out_ref, grad_ref, lo_v, a_v, x_v, c_v, cb_v, in_s, out_s):
    last = lax.rem(lax.axis_index("section"), PLANES) == PLANES - 1

    def columns(ref, h):
        return ref.at[:, pl.ds(h * HDIM, HDIM)]

    scalars_in = pltpu.make_async_copy(c_ref, c_v, in_s.at[3 * HEADS])
    scalars_in.start()
    arrivals = [
        [pltpu.make_async_copy(src.at[h], dst.at[h], in_s.at[k * HEADS + h])
         for k, (src, dst) in enumerate(((lo_ref, lo_v), (a_ref, a_v), (x_ref, x_v))) if k < 2 or h < EARLY]
        for h in range(HEADS)
    ]
    for copies in arrivals:
        for c in copies:
            c.start()
    scalars_in.wait()
    spread_columns(c_v[...], cb_v)
    leaving = []
    for h in range(HEADS):
        for c in arrivals[h]:
            c.wait()
        passed_on = pltpu.make_async_copy(lo_v.at[h], columns(out_ref, h), out_s.at[h])
        passed_on.start()
        leaving.append(passed_on)

        if h < EARLY:
            @pl.when(jnp.logical_not(last))
            def _():
                value = a_v[h].astype(jnp.float32) - x_v[h].astype(jnp.float32) * cb_v[...]
                a_v[h] = value.astype(jnp.bfloat16)

        made = pltpu.make_async_copy(a_v.at[h], columns(grad_ref, h), out_s.at[HEADS + h])
        made.start()
        leaving.append(made)
    for c in leaving:
        c.wait()


def local(layer_input, grad_input, stashed, eviction, query_gain, key_gain):
    head_buffer = pltpu.VMEM((HEADS, SEQ, HDIM), jnp.bfloat16)
    share_buffer = pltpu.VMEM((HEADS, WIDEST, HDIM), jnp.bfloat16)
    column = pltpu.VMEM((SEQ, HDIM), jnp.float32)
    gain = pltpu.VMEM((1, HEADS * HDIM), jnp.float32)
    tile = pltpu.VMEM((8, LANES), jnp.float32)
    row = pltpu.VMEM((1, SEQ), jnp.float32)
    dma = pltpu.SemaphoreType.DMA
    anywhere = pl.BlockSpec(memory_space=pl.ANY)
    flat = jax.ShapeDtypeStruct((SEQ, HEADS * HDIM), jnp.bfloat16)
    split = jax.ShapeDtypeStruct((HEADS, SEQ, HDIM), jnp.bfloat16)
    lo, a, x, c = pl.pallas_call(
        kernel,
        out_shape=(split, split, split, jax.ShapeDtypeStruct((1, SEQ), jnp.float32)),
        in_specs=[pl.BlockSpec(memory_space=pltpu.SMEM)] + [anywhere] * 5,
        out_specs=(anywhere,) * 4,
        scratch_shapes=[gain, gain] + [head_buffer] * 8 + [column] * 3 + [share_buffer] * 4 + [
            row,
            pltpu.VMEM((16, LANES), jnp.float32), pltpu.VMEM((GROUP, 16, LANES), jnp.float32),
            tile, tile, row, pltpu.VMEM((GROUP, 1, SEQ), jnp.float32), row, column, column,
            pltpu.SemaphoreType.REGULAR, pltpu.SemaphoreType.REGULAR,
        ] + [dma((HEADS,))] * 14 + [dma((GROUP,))] * 4 + [dma] * 5
        + [dma((len(SHARES), HEADS))] * 2 + [dma((len(SHARES),))] + [dma((CHUNKS,))] * 4,
        compiler_params=pltpu.CompilerParams(collective_id=0, has_side_effects=True, vmem_limit_bytes=60 * 2**20),
        name="tick",
    )(eviction, layer_input[0], grad_input[0], stashed[0], query_gain, key_gain)
    output, passed = pl.pallas_call(
        finish,
        out_shape=(flat, flat),
        in_specs=[anywhere] * 4,
        out_specs=(anywhere, anywhere),
        scratch_shapes=[head_buffer] * 3 + [row, column, dma((3 * HEADS + 1,)), dma((2 * HEADS,))],
        compiler_params=pltpu.CompilerParams(vmem_limit_bytes=60 * 2**20),
        name="finish",
    )(lo, a, x, c)
    return (output[None], passed[None])


def solution(mesh):
    placed = (
        P("section", None, "tensor"),
        P("section", None, "tensor"),
        P("section", None, None, "tensor"),
        P("section"),
        P("section", "tensor"),
        P("section", "tensor"),
    )
    return jax.shard_map(
        local,
        mesh=mesh,
        in_specs=placed,
        out_specs=(P("section", None, "tensor"), P("section", None, "tensor")),
        check_vma=False,
    )
```

```python
import functools
import math

import jax
import jax.numpy as jnp
from jax import lax
from jax.experimental import pallas as pl
from jax.experimental.pallas import tpu as pltpu
from jax.sharding import PartitionSpec as P

MESH = pl.DeviceIdType.MESH
HDIM = 128
SEQ = 512
DW = 6144
SECTIONS = 48
PLANES = 12
GROUP = 16
HEADS = 3
EARLY = HEADS - 1
BLOCK = 128
LANES = 128

CHUNK = 64
SHARES = ((0, 3), (3, 3), (6, 2))
WIDEST = 3 * CHUNK
CHUNKS = SEQ // CHUNK
EPSILON = 1e-05
SCALE = 1.0 / math.sqrt(HDIM)
EXPONENT = SCALE * math.log2(math.e)
NT = (((1,), (1,)), ((), ()))
TN = (((0,), (0,)), ((), ()))
NN = (((1,), (0,)), ((), ()))


def dot(a, b, dims):
    return lax.dot_general(a, b, dims, preferred_element_type=jnp.float32)


def row_sums(values):
    high = values.astype(jnp.bfloat16)
    low = (values - high.astype(jnp.float32)).astype(jnp.bfloat16)
    ones = jnp.ones((8, values.shape[-1]), jnp.bfloat16)
    return (dot(ones, high, NT) + dot(ones, low, NT))[0:1]


def spread_columns(row, out_ref):
    for lo in range(0, row.shape[1], LANES):
        block = jnp.broadcast_to(row[:, lo : lo + LANES], (LANES, LANES))
        out_ref[pl.ds(lo, LANES), :] = block.T


def block_weights(keys, queries, lo, hi):
    scores = dot(keys[:hi], queries[lo:hi], NT)
    width = hi - lo
    tail = scores[lo:]
    u = lax.broadcasted_iota(jnp.int32, (width, width), 0)
    t = lax.broadcasted_iota(jnp.int32, (width, width), 1)
    tail = jnp.where(u <= t, tail, -1e30)
    scores = tail if lo == 0 else jnp.concatenate([scores[:lo], tail], axis=0)
    top = jnp.max(scores, axis=0, keepdims=True)
    exponent = jnp.exp2((scores - top) * EXPONENT)
    return exponent * (1.0 / jnp.sum(exponent, axis=0, keepdims=True))


def kernel(
    ev_ref, li_ref, g_ref, st_ref, gq_ref, gk_ref,
    lo_ref, a_ref, x_ref, c_ref,
    gq_v, gk_v, li_v, g_v, own_v, away_v, got_v, x_v, a_v, lo_v, dq_v, dk_v, dv_v, dx_v, hop_v, rx_v, ra_v, rc_v,
    part_v, parts_v, extra_v, theirs_v, inner_v, inners_v, c_v, fb_v, cb_v,
    ready, opened, small_s, li_s, g_s, own_s, away_s, lo_s, stash_ss, stash_rs,
    a_ss, a_rs, x_ss, x_rs, wa_ss, wa_rs, wx_ss, wx_rs, sq_ss, sq_rs, in_ss, in_rs, ex_ss, ex_rs,
    c_ss, c_rs, wc_ss, wc_rs, dx_ss, dx_rs, hop_ss, hop_rs,
):
    s, t = lax.axis_index("section"), lax.axis_index("tensor")
    z = lax.rem(s, PLANES)
    first, last = z == 0, z == PLANES - 1
    inland = jnp.logical_not(first)

    def section(by):
        return lax.rem(s + (by + SECTIONS), SECTIONS)

    def remote(src, dst, ss, rs, to_s, to_t):
        return pltpu.make_async_remote_copy(
            src_ref=src, dst_ref=dst, send_sem=ss, recv_sem=rs,
            device_id={"section": to_s, "tensor": to_t}, device_id_type=MESH)

    def settle(ref, semaphore):
        pltpu.make_async_copy(ref, ref, semaphore).wait()

    def arrived(ref, semaphore):
        remote(ref, ref, semaphore, semaphore, section(1), t).wait_recv()

    def sent(ref, semaphore):
        remote(ref, ref, semaphore, semaphore, section(1), t).wait_send()

    barrier = pltpu.get_barrier_semaphore()

    def greet(to_s, to_t, semaphore=barrier):
        pl.semaphore_signal(semaphore, inc=1, device_id={"section": to_s, "tensor": to_t}, device_id_type=MESH)

    second, porter = z == 1, z >= PLANES - len(SHARES)
    outer = jnp.logical_and(porter, jnp.logical_not(last))
    greet(section(SECTIONS // 2), t)
    for by in range(1, GROUP):
        greet(s, lax.rem(t + by, GROUP))

    @pl.when(jnp.logical_and(inland, jnp.logical_not(last)))
    def _():
        greet(section(1), t)

    @pl.when(second)
    def _():
        greet(section(-1), t)

    @pl.when(first)
    def _():
        for k in range(len(SHARES)):
            greet(section(PLANES - 1 - k), t)

    @pl.when(porter)
    def _():
        greet(section(PLANES), t)

    @pl.when(last)
    def _():
        for k in range(1, len(SHARES)):
            greet(section(-k), t)

    def heads_in(src, dst, sems):
        return [pltpu.make_async_copy(src.at[:, pl.ds(h * HDIM, HDIM)], dst.at[h], sems) for h in range(HEADS)]

    away_in = heads_in(st_ref.at[1], away_v, away_s)
    li_in = heads_in(li_ref, li_v, li_s)
    own_in = heads_in(st_ref.at[0], own_v, own_s)
    g_in = heads_in(g_ref, g_v, g_s)
    small_in = [
        pltpu.make_async_copy(gq_ref, gq_v, small_s.at[0]),
        pltpu.make_async_copy(gk_ref, gk_v, small_s.at[1]),
    ]
    for c in away_in + li_in + own_in + small_in + g_in:
        c.start()

    def count(condition):
        return condition.astype(jnp.int32)

    @pl.when(porter)
    def _():
        pl.semaphore_wait(barrier, GROUP + 3 + count(outer))
        greet(lax.rem(s - z + SECTIONS, SECTIONS), t, ready)

    def squares(ref, slot):
        total = jnp.zeros((1, SEQ), jnp.float32)
        for h in range(HEADS):
            wide = ref[h].astype(jnp.float32)
            total = total + row_sums(wide * wide)
        part_v[:, slot * SEQ : (slot + 1) * SEQ] = total

    settle(away_v, away_s)
    squares(away_v, 2)
    settle(li_v, li_s)
    squares(li_v, 0)
    settle(own_v, own_s)
    squares(own_v, 1)

    @pl.when(jnp.logical_not(porter))
    def _():
        pl.semaphore_wait(barrier, GROUP + count(z != 1))

    @pl.when(first)
    def _():
        greet(section(1), t, opened)

    def stash(h):
        return remote(away_v.at[h], got_v.at[h], stash_ss, stash_rs.at[h], section(SECTIONS // 2), t)

    shares = [remote(part_v, parts_v.at[i], sq_ss, sq_rs, s, lax.rem(t + i, GROUP)) for i in range(1, GROUP)]
    for c in shares:
        c.start()
    stash(0).start()
    for c in small_in:
        c.wait()
    settle(g_v, g_s)
    others = pl.ds(1, GROUP - 1)
    arrived(parts_v.at[others], sq_rs)
    totals = part_v[...]
    for i in range(1, GROUP):
        totals = totals + parts_v[i]
    extra_v[...] = totals[:, 2 * SEQ :]
    extra = remote(extra_v, theirs_v, ex_ss, ex_rs, section(SECTIONS // 2), t)
    extra.start()
    stash(1).start()
    stash(2).start()

    def factor_of(total):
        return lax.rsqrt(total / DW + EPSILON)

    spread_columns(factor_of(totals[:, :SEQ]), fb_v)

    def forward(h, carry):
        cols = pl.ds(pl.multiple_of(h * HDIM, HDIM), HDIM)
        wide = li_v[h].astype(jnp.float32)
        normed = wide * fb_v[...]
        queries = (normed * gq_v[:, cols]).astype(jnp.bfloat16)
        keys = (normed * gk_v[:, cols]).astype(jnp.bfloat16)
        values = normed.astype(jnp.bfloat16)
        for lo in range(0, SEQ, BLOCK):
            hi = lo + BLOCK
            weights = block_weights(keys, queries, lo, hi).astype(jnp.bfloat16)
            mixed = dot(weights, values[:hi], TN)
            lo_v[h, pl.ds(lo, BLOCK), :] = (wide[lo:hi] + mixed).astype(jnp.bfloat16)
        pltpu.make_async_copy(lo_v.at[h], lo_ref.at[h], lo_s).start()
        return carry

    lax.fori_loop(0, HEADS, forward, 0)

    picked = jnp.full((SEQ, HDIM), ev_ref[0], jnp.int32) == 1

    def send_x(h):
        return remote(x_v.at[h], x_ref.at[h], x_ss, x_rs, section(-1), t)

    def send_a(h):
        return remote(a_v.at[h], a_ref.at[h], a_ss, a_rs, section(-1), t)

    def wrap_x(h, k):
        start, count = SHARES[k]
        rows, held = pl.ds(start * CHUNK, count * CHUNK), pl.ds(0, count * CHUNK)
        return remote(x_v.at[h, rows], rx_v.at[h, held], wx_ss, wx_rs, section(PLANES - 1 - k), t)

    def wrap_a(h, k):
        start, count = SHARES[k]
        rows, held = pl.ds(start * CHUNK, count * CHUNK), pl.ds(0, count * CHUNK)
        return remote(a_v.at[h, rows], ra_v.at[h, held], wa_ss, wa_rs, section(PLANES - 1 - k), t)

    def share_in(i):
        return remote(inner_v, inners_v.at[i], in_ss, in_rs, s, lax.rem(t + i, GROUP))

    send_c = remote(c_v, c_ref, c_ss, c_rs, section(-1), t)

    def wrap_c(k):
        return remote(c_v, rc_v, wc_ss, wc_rs, section(PLANES - 1 - k), t)

    def pass_on(whole, halves, h):
        @pl.when(inland)
        def _():
            whole(h).start()

        @pl.when(first)
        def _():
            for k in range(len(SHARES)):
                halves(h, k).start()

    def choose(h):
        stash(h).wait_recv()
        wide = jnp.where(picked, got_v[h].astype(jnp.float32), own_v[h].astype(jnp.float32))
        x_v[h] = wide.astype(jnp.bfloat16)

        @pl.when(h < EARLY)
        def _():
            pass_on(send_x, wrap_x, h)

    @pl.when(second)
    def _():
        pl.semaphore_wait(opened, 1)

    @pl.when(first)
    def _():
        pl.semaphore_wait(ready, len(SHARES))

    choose(0)
    extra.wait_recv()
    evicted = jnp.full((1, SEQ), ev_ref[0], jnp.int32) == 1
    f = factor_of(jnp.where(evicted, theirs_v[...], totals[:, SEQ : 2 * SEQ]))
    spread_columns(f, fb_v)

    def backward(h, partial):
        cols = pl.ds(pl.multiple_of(h * HDIM, HDIM), HDIM)
        wide = x_v[h].astype(jnp.float32)
        normed = wide * fb_v[...]
        gq, gk = gq_v[:, cols], gk_v[:, cols]
        queries = (normed * gq).astype(jnp.bfloat16)
        keys = (normed * gk).astype(jnp.bfloat16)
        values = normed.astype(jnp.bfloat16)
        grads = g_v[h]
        for lo in range(SEQ - BLOCK, -1, -BLOCK):
            hi = lo + BLOCK
            weights = block_weights(keys, queries, lo, hi)
            d_weights = dot(values[:hi], grads[lo:hi], NT)
            delta = jnp.sum(weights * d_weights, axis=0, keepdims=True)
            d_scores = (weights * (d_weights - delta) * SCALE).astype(jnp.bfloat16)
            d_keys = dot(d_scores, queries[lo:hi], NN)
            d_values = dot(weights.astype(jnp.bfloat16), grads[lo:hi], NN)
            if hi == SEQ:
                dk_v[...] = d_keys
                dv_v[...] = d_values
            else:
                dk_v[0:hi] += d_keys
                dv_v[0:hi] += d_values
            dq_v[pl.ds(lo, BLOCK), :] = dot(d_scores, keys[:hi], TN) * gq
        d_normed = dq_v[...] + dk_v[...] * gk + dv_v[...]
        a32 = grads.astype(jnp.float32) + fb_v[...] * d_normed
        dq_v[...] = a32

        @pl.when(h < EARLY)
        def _():
            a_v[h] = a32.astype(jnp.bfloat16)
            pass_on(send_a, wrap_a, h)
            choose(h + 1)

        return partial + row_sums(d_normed * wide)

    partial = lax.fori_loop(0, HEADS, backward, jnp.zeros((1, SEQ), jnp.float32))
    inner_v[...] = partial * (f * f * f * (1.0 / DW))
    for i in range(1, GROUP):
        share_in(i).start()

    def rows_at(c):
        return pl.ds(c * CHUNK, CHUNK)

    def carry(c):
        return remote(dx_v.at[:, rows_at(c)], a_ref.at[:, rows_at(c)], dx_ss, dx_rs, section(-PLANES), t)

    def leg(c):
        return remote(dx_v.at[:, rows_at(c)], hop_v.at[:, rows_at(c)], dx_ss, hop_rs.at[c], section(-PLANES), t)

    def land(c, k):
        at = SHARES[k][0] + c
        return remote(hop_v.at[:, rows_at(c)], a_ref.at[:, rows_at(at)], hop_ss, dx_rs, section(k), t)

    @pl.when(porter)
    def _():
        wrap_c(0).wait_recv()
        spread_columns(rc_v[...], cb_v)
        for k, (start, chunks) in enumerate(SHARES):
            @pl.when(z == PLANES - 1 - k)
            def _():
                arrived(rx_v.at[pl.ds(0, EARLY), pl.ds(0, chunks * CHUNK)], wx_rs)
                arrived(ra_v.at[:, pl.ds(0, chunks * CHUNK)], wa_rs)
                for c in range(chunks):
                    rows, tokens = rows_at(c), rows_at(start + c)
                    dx_v[EARLY, rows, :] = ra_v[EARLY, rows, :]
                    for h in range(EARLY):
                        value = ra_v[h, rows, :].astype(jnp.float32) - rx_v[h, rows, :].astype(jnp.float32) * cb_v[tokens, :]
                        dx_v[h, rows, :] = value.astype(jnp.bfloat16)
                    (leg(c) if k else carry(c)).start()

    arrived(inners_v.at[others], in_rs)
    scalars = inner_v[...]
    for i in range(1, GROUP):
        scalars = scalars + inners_v[i]
    c_v[...] = scalars

    @pl.when(inland)
    def _():
        send_c.start()

    @pl.when(first)
    def _():
        for k in range(len(SHARES)):
            wrap_c(k).start()

    spread_columns(scalars, cb_v)
    a_v[EARLY] = (dq_v[...] - x_v[EARLY].astype(jnp.float32) * cb_v[...]).astype(jnp.bfloat16)
    pass_on(send_a, wrap_a, EARLY)

    @pl.when(outer)
    def _():
        for k in range(1, len(SHARES)):
            @pl.when(z == PLANES - 1 - k)
            def _():
                for c in range(SHARES[k][1]):
                    leg(c).wait_recv()
                    land(c, k).start()
                rows = pl.ds(0, SHARES[k][1] * CHUNK)
                sent(dx_v.at[:, rows], dx_ss)
                sent(hop_v.at[:, rows], hop_ss)

    @pl.when(last)
    def _():
        sent(dx_v.at[:, pl.ds(0, SHARES[0][1] * CHUNK)], dx_ss)

    @pl.when(last)
    def _():
        arrived(a_ref, dx_rs)

    @pl.when(first)
    def _():
        sent(x_ref, wx_ss)
        sent(a_v, wa_ss)
        sent(inners_v.at[pl.ds(0, len(SHARES))], wc_ss)

    @pl.when(inland)
    def _():
        sent(x_ref, x_ss)
        sent(a_v, a_ss)
        send_c.wait_send()

    sent(away_v, stash_ss)
    settle(lo_v, lo_s)
    sent(parts_v.at[others], sq_ss)
    sent(inners_v.at[others], in_ss)
    extra.wait_send()

    @pl.when(jnp.logical_not(last))
    def _():
        arrived(x_ref, x_rs)
        arrived(a_ref, a_rs)
        send_c.wait_recv()


def finish(lo_ref, a_ref, x_ref, c_ref, out_ref, grad_ref, lo_v, a_v, x_v, c_v, cb_v, in_s, out_s):
    last = lax.rem(lax.axis_index("section"), PLANES) == PLANES - 1

    def columns(ref, h):
        return ref.at[:, pl.ds(h * HDIM, HDIM)]

    scalars_in = pltpu.make_async_copy(c_ref, c_v, in_s.at[3 * HEADS])
    scalars_in.start()
    arrivals = [
        [pltpu.make_async_copy(src.at[h], dst.at[h], in_s.at[k * HEADS + h])
         for k, (src, dst) in enumerate(((lo_ref, lo_v), (a_ref, a_v), (x_ref, x_v))) if k < 2 or h < EARLY]
        for h in range(HEADS)
    ]
    for copies in arrivals:
        for c in copies:
            c.start()
    scalars_in.wait()
    spread_columns(c_v[...], cb_v)
    leaving = []
    for h in range(HEADS):
        for c in arrivals[h]:
            c.wait()
        passed_on = pltpu.make_async_copy(lo_v.at[h], columns(out_ref, h), out_s.at[h])
        passed_on.start()
        leaving.append(passed_on)

        if h < EARLY:
            @pl.when(jnp.logical_not(last))
            def _():
                value = a_v[h].astype(jnp.float32) - x_v[h].astype(jnp.float32) * cb_v[...]
                a_v[h] = value.astype(jnp.bfloat16)

        made = pltpu.make_async_copy(a_v.at[h], columns(grad_ref, h), out_s.at[HEADS + h])
        made.start()
        leaving.append(made)
    for c in leaving:
        c.wait()


def local(layer_input, grad_input, stashed, eviction, query_gain, key_gain):
    head_buffer = pltpu.VMEM((HEADS, SEQ, HDIM), jnp.bfloat16)
    share_buffer = pltpu.VMEM((HEADS, WIDEST, HDIM), jnp.bfloat16)
    column = pltpu.VMEM((SEQ, HDIM), jnp.float32)
    gain = pltpu.VMEM((1, HEADS * HDIM), jnp.float32)
    row = pltpu.VMEM((1, SEQ), jnp.float32)
    dma = pltpu.SemaphoreType.DMA
    anywhere = pl.BlockSpec(memory_space=pl.ANY)
    flat = jax.ShapeDtypeStruct((SEQ, HEADS * HDIM), jnp.bfloat16)
    split = jax.ShapeDtypeStruct((HEADS, SEQ, HDIM), jnp.bfloat16)
    early = jax.ShapeDtypeStruct((EARLY, SEQ, HDIM), jnp.bfloat16)
    lo, a, x, c = pl.pallas_call(
        kernel,
        out_shape=(split, split, early, jax.ShapeDtypeStruct((1, SEQ), jnp.float32)),
        in_specs=[pl.BlockSpec(memory_space=pltpu.SMEM)] + [anywhere] * 5,
        out_specs=(anywhere,) * 4,
        scratch_shapes=[gain, gain] + [head_buffer] * 8 + [column] * 3 + [share_buffer] * 4 + [
            row,
            pltpu.VMEM((1, 3 * SEQ), jnp.float32), pltpu.VMEM((GROUP, 1, 3 * SEQ), jnp.float32),
            row, row, row, pltpu.VMEM((GROUP, 1, SEQ), jnp.float32), row, column, column,
            pltpu.SemaphoreType.REGULAR, pltpu.SemaphoreType.REGULAR,
        ] + [dma((2,))] + [dma] * 6 + [dma((HEADS,))] + [dma] * 21 + [dma((SHARES[0][1],))],
        compiler_params=pltpu.CompilerParams(collective_id=0, has_side_effects=True, vmem_limit_bytes=60 * 2**20),
        name="tick",
    )(eviction, layer_input[0], grad_input[0], stashed[0], query_gain, key_gain)
    output, passed = pl.pallas_call(
        finish,
        out_shape=(flat, flat),
        in_specs=[anywhere] * 4,
        out_specs=(anywhere, anywhere),
        scratch_shapes=[head_buffer] * 3 + [row, column, dma((3 * HEADS + 1,)), dma((2 * HEADS,))],
        compiler_params=pltpu.CompilerParams(vmem_limit_bytes=60 * 2**20),
        name="finish",
    )(lo, a, x, c)
    return (output[None], passed[None])


def solution(mesh):
    placed = (
        P("section", None, "tensor"),
        P("section", None, "tensor"),
        P("section", None, None, "tensor"),
        P("section"),
        P("section", "tensor"),
        P("section", "tensor"),
    )
    return jax.shard_map(
        local,
        mesh=mesh,
        in_specs=placed,
        out_specs=(P("section", None, "tensor"), P("section", None, "tensor")),
        check_vma=False,
    )
```

```python
import functools
import math

import jax
import jax.numpy as jnp
from jax import lax
from jax.experimental import pallas as pl
from jax.experimental.pallas import tpu as pltpu
from jax.sharding import PartitionSpec as P

MESH = pl.DeviceIdType.MESH
HDIM = 128
SEQ = 512
DW = 6144
SECTIONS = 48
PLANES = 12
GROUP = 16
HEADS = 3
EARLY = HEADS - 1
BLOCK = 128
LANES = 128

CHUNK = 64
SHARES = ((0, 4), (4, 2), (6, 2))
WIDEST = 4 * CHUNK
HALF = SEQ // 2
CHUNKS = SEQ // CHUNK
EPSILON = 1e-05
SCALE = 1.0 / math.sqrt(HDIM)
EXPONENT = SCALE * math.log2(math.e)
NT = (((1,), (1,)), ((), ()))
TN = (((0,), (0,)), ((), ()))
NN = (((1,), (0,)), ((), ()))


def dot(a, b, dims):
    return lax.dot_general(a, b, dims, preferred_element_type=jnp.float32)


def row_sums(values):
    high = values.astype(jnp.bfloat16)
    low = (values - high.astype(jnp.float32)).astype(jnp.bfloat16)
    ones = jnp.ones((8, values.shape[-1]), jnp.bfloat16)
    return (dot(ones, high, NT) + dot(ones, low, NT))[0:1]


def spread_columns(row, out_ref):
    for lo in range(0, row.shape[1], LANES):
        block = jnp.broadcast_to(row[:, lo : lo + LANES], (LANES, LANES))
        out_ref[pl.ds(lo, LANES), :] = block.T


def block_weights(keys, queries, lo, hi):
    scores = dot(keys[:hi], queries[lo:hi], NT)
    width = hi - lo
    tail = scores[lo:]
    u = lax.broadcasted_iota(jnp.int32, (width, width), 0)
    t = lax.broadcasted_iota(jnp.int32, (width, width), 1)
    tail = jnp.where(u <= t, tail, -1e30)
    scores = tail if lo == 0 else jnp.concatenate([scores[:lo], tail], axis=0)
    top = jnp.max(scores, axis=0, keepdims=True)
    exponent = jnp.exp2((scores - top) * EXPONENT)
    return exponent * (1.0 / jnp.sum(exponent, axis=0, keepdims=True))


def kernel(
    ev_ref, li_ref, g_ref, st_ref, gq_ref, gk_ref,
    lo_ref, a_ref, x_ref, c_ref,
    gq_v, gk_v, li_v, g_v, own_v, away_v, got_v, x_v, a_v, lo_v, dq_v, dk_v, dv_v, dx_v, hop_v, rx_v, ra_v, rc_v,
    part_v, parts_v, extra_v, theirs_v, inner_v, inners_v, c_v, fb_v, cb_v,
    ready, opened, small_s, li_s, g_s, own_s, away_s, lo_s, stash_ss, stash_rs,
    a_ss, a_rs, x_ss, x_rs, wa_ss, wa_rs, wx_ss, wx_rs, sq_ss, sq_rs, in_ss, in_rs, ex_ss, ex_rs,
    c_ss, c_rs, wc_ss, wc_rs, wl_ss, dx_ss, dx_rs, hop_ss, hop_rs,
):
    s, t = lax.axis_index("section"), lax.axis_index("tensor")
    z = lax.rem(s, PLANES)
    first, last = z == 0, z == PLANES - 1
    inland = jnp.logical_not(first)

    def section(by):
        return lax.rem(s + (by + SECTIONS), SECTIONS)

    def remote(src, dst, ss, rs, to_s, to_t):
        return pltpu.make_async_remote_copy(
            src_ref=src, dst_ref=dst, send_sem=ss, recv_sem=rs,
            device_id={"section": to_s, "tensor": to_t}, device_id_type=MESH)

    def settle(ref, semaphore):
        pltpu.make_async_copy(ref, ref, semaphore).wait()

    def arrived(ref, semaphore):
        remote(ref, ref, semaphore, semaphore, section(1), t).wait_recv()

    def sent(ref, semaphore):
        remote(ref, ref, semaphore, semaphore, section(1), t).wait_send()

    barrier = pltpu.get_barrier_semaphore()

    def greet(to_s, to_t, semaphore=barrier):
        pl.semaphore_signal(semaphore, inc=1, device_id={"section": to_s, "tensor": to_t}, device_id_type=MESH)

    second, porter = z == 1, z >= PLANES - len(SHARES)
    outer = jnp.logical_and(porter, jnp.logical_not(last))
    greet(section(SECTIONS // 2), t)
    for by in range(1, GROUP):
        greet(s, lax.rem(t + by, GROUP))

    @pl.when(jnp.logical_and(inland, jnp.logical_not(last)))
    def _():
        greet(section(1), t)

    @pl.when(second)
    def _():
        greet(section(-1), t)

    @pl.when(first)
    def _():
        for k in range(len(SHARES)):
            greet(section(PLANES - 1 - k), t)

    @pl.when(porter)
    def _():
        greet(section(PLANES), t)

    @pl.when(last)
    def _():
        for k in range(1, len(SHARES)):
            greet(section(-k), t)

    def heads_in(src, dst, sems):
        return [pltpu.make_async_copy(src.at[:, pl.ds(h * HDIM, HDIM)], dst.at[h], sems) for h in range(HEADS)]

    away_in = heads_in(st_ref.at[1], away_v, away_s)
    li_in = heads_in(li_ref, li_v, li_s)
    own_in = heads_in(st_ref.at[0], own_v, own_s)
    g_in = heads_in(g_ref, g_v, g_s)
    small_in = [
        pltpu.make_async_copy(gq_ref, gq_v, small_s.at[0]),
        pltpu.make_async_copy(gk_ref, gk_v, small_s.at[1]),
    ]
    for c in away_in + li_in + own_in + small_in + g_in:
        c.start()

    def count(condition):
        return condition.astype(jnp.int32)

    @pl.when(porter)
    def _():
        pl.semaphore_wait(barrier, GROUP + 3 + count(outer))
        greet(lax.rem(s - z + SECTIONS, SECTIONS), t, ready)

    def squares(ref, slot):
        total = jnp.zeros((1, SEQ), jnp.float32)
        for h in range(HEADS):
            wide = ref[h].astype(jnp.float32)
            total = total + row_sums(wide * wide)
        part_v[:, slot * SEQ : (slot + 1) * SEQ] = total

    settle(away_v, away_s)
    squares(away_v, 2)
    settle(li_v, li_s)
    squares(li_v, 0)
    settle(own_v, own_s)
    squares(own_v, 1)

    @pl.when(jnp.logical_not(porter))
    def _():
        pl.semaphore_wait(barrier, GROUP + count(z != 1))

    @pl.when(first)
    def _():
        greet(section(1), t, opened)

    def stash(h):
        return remote(away_v.at[h], got_v.at[h], stash_ss, stash_rs.at[h], section(SECTIONS // 2), t)

    shares = [remote(part_v, parts_v.at[i], sq_ss, sq_rs, s, lax.rem(t + i, GROUP)) for i in range(1, GROUP)]
    for c in shares:
        c.start()
    stash(0).start()
    for c in small_in:
        c.wait()
    settle(g_v, g_s)
    others = pl.ds(1, GROUP - 1)
    arrived(parts_v.at[others], sq_rs)
    totals = part_v[...]
    for i in range(1, GROUP):
        totals = totals + parts_v[i]
    extra_v[...] = totals[:, 2 * SEQ :]
    extra = remote(extra_v, theirs_v, ex_ss, ex_rs, section(SECTIONS // 2), t)
    extra.start()
    stash(1).start()
    stash(2).start()

    def factor_of(total):
        return lax.rsqrt(total / DW + EPSILON)

    spread_columns(factor_of(totals[:, :SEQ]), fb_v)

    def forward(h, carry):
        cols = pl.ds(pl.multiple_of(h * HDIM, HDIM), HDIM)
        wide = li_v[h].astype(jnp.float32)
        normed = wide * fb_v[...]
        queries = (normed * gq_v[:, cols]).astype(jnp.bfloat16)
        keys = (normed * gk_v[:, cols]).astype(jnp.bfloat16)
        values = normed.astype(jnp.bfloat16)
        for lo in range(0, SEQ, BLOCK):
            hi = lo + BLOCK
            weights = block_weights(keys, queries, lo, hi).astype(jnp.bfloat16)
            mixed = dot(weights, values[:hi], TN)
            lo_v[h, pl.ds(lo, BLOCK), :] = (wide[lo:hi] + mixed).astype(jnp.bfloat16)
        pltpu.make_async_copy(lo_v.at[h], lo_ref.at[h], lo_s).start()
        return carry

    lax.fori_loop(0, HEADS, forward, 0)

    picked = jnp.full((SEQ, HDIM), ev_ref[0], jnp.int32) == 1

    upper, lower = pl.ds(0, HALF), pl.ds(HALF, HALF)

    def send_x(h, k):
        rows = (upper, lower)[k]
        return remote(x_v.at[h, rows], x_ref.at[2 * h + k], x_ss, x_rs, section(-1), t)

    def send_a(h, rows):
        return remote(a_v.at[h, rows], a_ref.at[h, rows], a_ss, a_rs, section(-1), t)

    def wrap_x(h, k, semaphore=wx_ss):
        start, count = SHARES[k]
        rows, held = pl.ds(start * CHUNK, count * CHUNK), pl.ds(0, count * CHUNK)
        return remote(x_v.at[h, rows], rx_v.at[h, held], semaphore, wx_rs, section(PLANES - 1 - k), t)

    def wrap_a(h, k):
        start, count = SHARES[k]
        rows, held = pl.ds(start * CHUNK, count * CHUNK), pl.ds(0, count * CHUNK)
        return remote(a_v.at[h, rows], ra_v.at[h, held], wa_ss, wa_rs, section(PLANES - 1 - k), t)

    def share_in(i):
        return remote(inner_v, inners_v.at[i], in_ss, in_rs, s, lax.rem(t + i, GROUP))

    send_c = remote(c_v, c_ref, c_ss, c_rs, section(-1), t)

    def wrap_c(k):
        return remote(c_v, rc_v, wc_ss, wc_rs, section(PLANES - 1 - k), t)

    def to_porters(piece, h):
        @pl.when(first)
        def _():
            for k in range(len(SHARES)):
                piece(h, k).start()

    def choose(h):
        stash(h).wait_recv()
        wide = jnp.where(picked, got_v[h].astype(jnp.float32), own_v[h].astype(jnp.float32))
        x_v[h] = wide.astype(jnp.bfloat16)

        @pl.when(inland)
        def _():
            send_x(h, 0).start()

        @pl.when(h < EARLY)
        def _():
            to_porters(wrap_x, h)

            @pl.when(inland)
            def _():
                send_x(h, 1).start()

        @pl.when(jnp.logical_and(first, h == EARLY))
        def _():
            wrap_x(EARLY, 0, wl_ss).start()

    @pl.when(second)
    def _():
        pl.semaphore_wait(opened, 1)

    @pl.when(first)
    def _():
        pl.semaphore_wait(ready, len(SHARES))

    choose(0)
    extra.wait_recv()
    evicted = jnp.full((1, SEQ), ev_ref[0], jnp.int32) == 1
    f = factor_of(jnp.where(evicted, theirs_v[...], totals[:, SEQ : 2 * SEQ]))
    spread_columns(f, fb_v)

    def backward(h, partial):
        cols = pl.ds(pl.multiple_of(h * HDIM, HDIM), HDIM)
        wide = x_v[h].astype(jnp.float32)
        normed = wide * fb_v[...]
        gq, gk = gq_v[:, cols], gk_v[:, cols]
        queries = (normed * gq).astype(jnp.bfloat16)
        keys = (normed * gk).astype(jnp.bfloat16)
        values = normed.astype(jnp.bfloat16)
        grads = g_v[h]
        for lo in range(SEQ - BLOCK, -1, -BLOCK):
            hi = lo + BLOCK
            weights = block_weights(keys, queries, lo, hi)
            d_weights = dot(values[:hi], grads[lo:hi], NT)
            delta = jnp.sum(weights * d_weights, axis=0, keepdims=True)
            d_scores = (weights * (d_weights - delta) * SCALE).astype(jnp.bfloat16)
            d_keys = dot(d_scores, queries[lo:hi], NN)
            d_values = dot(weights.astype(jnp.bfloat16), grads[lo:hi], NN)
            if hi == SEQ:
                dk_v[...] = d_keys
                dv_v[...] = d_values
            else:
                dk_v[0:hi] += d_keys
                dv_v[0:hi] += d_values
            dq_v[pl.ds(lo, BLOCK), :] = dot(d_scores, keys[:hi], TN) * gq
        d_normed = dq_v[...] + dk_v[...] * gk + dv_v[...]
        a32 = grads.astype(jnp.float32) + fb_v[...] * d_normed
        dq_v[...] = a32
        a_v[h] = a32.astype(jnp.bfloat16)

        @pl.when(inland)
        def _():
            send_a(h, upper).start()

        @pl.when(h < EARLY)
        def _():
            to_porters(wrap_a, h)

            @pl.when(inland)
            def _():
                send_a(h, lower).start()

        @pl.when(jnp.logical_and(first, h == EARLY))
        def _():
            wrap_a(EARLY, 0).start()

        @pl.when(h < EARLY)
        def _():
            choose(h + 1)

        return partial + row_sums(d_normed * wide)

    partial = lax.fori_loop(0, HEADS, backward, jnp.zeros((1, SEQ), jnp.float32))
    inner_v[...] = partial * (f * f * f * (1.0 / DW))
    for i in range(1, GROUP):
        share_in(i).start()

    def rows_at(c):
        return pl.ds(c * CHUNK, CHUNK)

    def carry(c):
        return remote(dx_v.at[:, rows_at(c)], a_ref.at[:, rows_at(c)], dx_ss, dx_rs, section(-PLANES), t)

    def leg(c):
        return remote(dx_v.at[:, rows_at(c)], hop_v.at[:, rows_at(c)], dx_ss, hop_rs.at[c], section(-PLANES), t)

    def land(c, k):
        at = SHARES[k][0] + c
        return remote(hop_v.at[:, rows_at(c)], a_ref.at[:, rows_at(at)], hop_ss, dx_rs, section(k), t)

    @pl.when(porter)
    def _():
        wrap_c(0).wait_recv()
        spread_columns(rc_v[...], cb_v)
        for k, (start, chunks) in enumerate(SHARES):
            @pl.when(z == PLANES - 1 - k)
            def _():
                paired = EARLY if k else HEADS
                arrived(rx_v.at[pl.ds(0, paired), pl.ds(0, chunks * CHUNK)], wx_rs)
                arrived(ra_v.at[:, pl.ds(0, chunks * CHUNK)], wa_rs)
                for c in range(chunks):
                    rows, tokens = rows_at(c), rows_at(start + c)
                    if k:
                        dx_v[EARLY, rows, :] = ra_v[EARLY, rows, :]
                    for h in range(paired):
                        value = ra_v[h, rows, :].astype(jnp.float32) - rx_v[h, rows, :].astype(jnp.float32) * cb_v[tokens, :]
                        dx_v[h, rows, :] = value.astype(jnp.bfloat16)
                    (leg(c) if k else carry(c)).start()

    arrived(inners_v.at[others], in_rs)
    scalars = inner_v[...]
    for i in range(1, GROUP):
        scalars = scalars + inners_v[i]
    c_v[...] = scalars

    @pl.when(inland)
    def _():
        send_c.start()

    @pl.when(first)
    def _():
        for k in range(len(SHARES)):
            wrap_c(k).start()

    spread_columns(scalars, cb_v)
    def complete(rows):
        value = dq_v[rows, :] - x_v[EARLY, rows, :].astype(jnp.float32) * cb_v[rows, :]
        a_v[EARLY, rows, :] = value.astype(jnp.bfloat16)

    @pl.when(inland)
    def _():
        complete(lower)
        send_a(EARLY, lower).start()

    @pl.when(first)
    def _():
        for k in range(1, len(SHARES)):
            start, chunks = SHARES[k]
            complete(pl.ds(start * CHUNK, chunks * CHUNK))
            wrap_a(EARLY, k).start()

    @pl.when(outer)
    def _():
        for k in range(1, len(SHARES)):
            @pl.when(z == PLANES - 1 - k)
            def _():
                for c in range(SHARES[k][1]):
                    leg(c).wait_recv()
                    land(c, k).start()
                rows = pl.ds(0, SHARES[k][1] * CHUNK)
                sent(dx_v.at[:, rows], dx_ss)
                sent(hop_v.at[:, rows], hop_ss)

    @pl.when(last)
    def _():
        sent(dx_v.at[:, pl.ds(0, SHARES[0][1] * CHUNK)], dx_ss)

    @pl.when(last)
    def _():
        arrived(a_ref, dx_rs)

    @pl.when(first)
    def _():
        sent(x_ref.at[pl.ds(0, 2 * EARLY)], wx_ss)
        wrap_x(EARLY, 0, wl_ss).wait_send()
        sent(a_v, wa_ss)
        sent(inners_v.at[pl.ds(0, len(SHARES))], wc_ss)

    @pl.when(inland)
    def _():
        sent(x_ref, x_ss)
        sent(a_v, a_ss)
        send_c.wait_send()

    sent(away_v, stash_ss)
    settle(lo_v, lo_s)
    sent(parts_v.at[others], sq_ss)
    sent(inners_v.at[others], in_ss)
    extra.wait_send()

    @pl.when(jnp.logical_not(last))
    def _():
        arrived(x_ref, x_rs)
        arrived(a_ref, a_rs)
        send_c.wait_recv()


def finish(lo_ref, a_ref, x_ref, c_ref, out_ref, grad_ref, lo_v, a_v, x_v, c_v, cb_v, in_s, out_s):
    last = lax.rem(lax.axis_index("section"), PLANES) == PLANES - 1

    def columns(ref, h):
        return ref.at[:, pl.ds(h * HDIM, HDIM)]

    scalars_in = pltpu.make_async_copy(c_ref, c_v, in_s.at[3 * HEADS])
    scalars_in.start()
    arrivals = []
    for h in range(HEADS):
        halves = pl.ds(2 * h, 2 if h < EARLY else 1)
        arrivals.append([
            pltpu.make_async_copy(lo_ref.at[h], lo_v.at[h], in_s.at[h]),
            pltpu.make_async_copy(a_ref.at[h], a_v.at[h], in_s.at[HEADS + h]),
            pltpu.make_async_copy(x_ref.at[halves], x_v.at[halves], in_s.at[2 * HEADS + h]),
        ])
    for copies in arrivals:
        for c in copies[1:]:
            c.start()
    for copies in arrivals:
        copies[0].start()
    leaving = []
    scalars_in.wait()
    spread_columns(c_v[...], cb_v)
    for h in range(HEADS):
        for c in arrivals[h][1:]:
            c.wait()

        @pl.when(jnp.logical_not(last))
        def _():
            for k in range(2 if h < EARLY else 1):
                rows = pl.ds(k * HALF, HALF)
                value = a_v[h, rows, :].astype(jnp.float32) - x_v[2 * h + k].astype(jnp.float32) * cb_v[rows, :]
                a_v[h, rows, :] = value.astype(jnp.bfloat16)

        made = pltpu.make_async_copy(a_v.at[h], columns(grad_ref, h), out_s.at[HEADS + h])
        made.start()
        arrivals[h][0].wait()
        passed_on = pltpu.make_async_copy(lo_v.at[h], columns(out_ref, h), out_s.at[h])
        passed_on.start()
        leaving += [made, passed_on]
    for c in leaving:
        c.wait()


def local(layer_input, grad_input, stashed, eviction, query_gain, key_gain):
    head_buffer = pltpu.VMEM((HEADS, SEQ, HDIM), jnp.bfloat16)
    share_buffer = pltpu.VMEM((HEADS, WIDEST, HDIM), jnp.bfloat16)
    column = pltpu.VMEM((SEQ, HDIM), jnp.float32)
    gain = pltpu.VMEM((1, HEADS * HDIM), jnp.float32)
    row = pltpu.VMEM((1, SEQ), jnp.float32)
    dma = pltpu.SemaphoreType.DMA
    anywhere = pl.BlockSpec(memory_space=pl.ANY)
    flat = jax.ShapeDtypeStruct((SEQ, HEADS * HDIM), jnp.bfloat16)
    split = jax.ShapeDtypeStruct((HEADS, SEQ, HDIM), jnp.bfloat16)
    early = jax.ShapeDtypeStruct((2 * EARLY + 1, HALF, HDIM), jnp.bfloat16)
    lo, a, x, c = pl.pallas_call(
        kernel,
        out_shape=(split, split, early, jax.ShapeDtypeStruct((1, SEQ), jnp.float32)),
        in_specs=[pl.BlockSpec(memory_space=pltpu.SMEM)] + [anywhere] * 5,
        out_specs=(anywhere,) * 4,
        scratch_shapes=[gain, gain] + [head_buffer] * 8 + [column] * 3 + [share_buffer] * 4 + [
            row,
            pltpu.VMEM((1, 3 * SEQ), jnp.float32), pltpu.VMEM((GROUP, 1, 3 * SEQ), jnp.float32),
            row, row, row, pltpu.VMEM((GROUP, 1, SEQ), jnp.float32), row, column, column,
            pltpu.SemaphoreType.REGULAR, pltpu.SemaphoreType.REGULAR,
        ] + [dma((2,))] + [dma] * 6 + [dma((HEADS,))] + [dma] * 22 + [dma((SHARES[0][1],))],
        compiler_params=pltpu.CompilerParams(collective_id=0, has_side_effects=True, vmem_limit_bytes=60 * 2**20),
        name="tick",
    )(eviction, layer_input[0], grad_input[0], stashed[0], query_gain, key_gain)
    output, passed = pl.pallas_call(
        finish,
        out_shape=(flat, flat),
        in_specs=[anywhere] * 4,
        out_specs=(anywhere, anywhere),
        scratch_shapes=[head_buffer] * 2 + [pltpu.VMEM((2 * EARLY + 1, HALF, HDIM), jnp.bfloat16), row, column, dma((3 * HEADS + 1,)), dma((2 * HEADS,))],
        compiler_params=pltpu.CompilerParams(vmem_limit_bytes=60 * 2**20),
        name="finish",
    )(lo, a, x, c)
    return (output[None], passed[None])


def solution(mesh):
    placed = (
        P("section", None, "tensor"),
        P("section", None, "tensor"),
        P("section", None, None, "tensor"),
        P("section"),
        P("section", "tensor"),
        P("section", "tensor"),
    )
    return jax.shard_map(
        local,
        mesh=mesh,
        in_specs=placed,
        out_specs=(P("section", None, "tensor"), P("section", None, "tensor")),
        check_vma=False,
    )
```
